32 devices in a mesh: front: 2 (over core), row: 4 (over y, x), col: 4 (over z).
Axes of the slice: x: 2, y: 2, z: 4, core: 2. Of those that a mesh axis runs over, the one named last changes fastest.
Arguments:
- child_blocks: bfloat16 [16384, 8192], P(('front', 'row'), 'col'), may hold values from -0.0625 to 0.0625
- sketch: bfloat16 [8192, 512], P('col'), may hold values from -6 to 6
- block_map: int32 [2, 64], P('front'), may hold values from 0 to 95, as said below
Outputs:
- parent_basis: float32 [512, 12288], P('col', ('front', 'row'))
The draws below stay inside these ranges and needn't reach their ends.
Inputs may be any that keep to these rules, and one draw needn't show every extreme that they name: `block_map`: each row lists 8192 / 128 different parent blocks in increasing order.
All inputs are finite; a program needn't handle non-finite values.
Results may differ from the reference program's by a relative error of at most 0.0003.
Values sent between devices are 32-bit elements; how exact they have to be, the bound alone decides.
No kernel may reach another device: no remote copies, remote signals or barrier semaphores. Data moves between devices by JAX's collectives and lax.ppermute only.
A program may use at most 128 MiB of HBM per device.

```python
import jax
import jax.numpy as jnp
from jax import lax

F = 8192
P_SIZE = 12288
S = 512
BLK = 128
R = 8192
CHILDREN = 2
SIBS = 2
PARENTS = 1


def draw_block_map(key, part):
    child_keys = jax.random.split(jax.random.fold_in(key, 7), CHILDREN)

    def one_child(child_key):
        chosen = jax.random.permutation(child_key, P_SIZE // BLK)[:R // BLK]
        return jnp.sort(chosen)
    return jax.vmap(one_child)(child_keys).astype(jnp.int32)


def shard_levels(stream_key, extent, shards, low, high):
    factor_of, own = 1.0, jax.random.fold_in(stream_key, 6)
    for axis_at, parts in shards:
        draws = jnp.exp(jax.random.uniform(jax.random.fold_in(own, axis_at), (parts,), jnp.float32, low / len(shards), high / len(shards)))
        factor_of = factor_of * jnp.repeat(draws, extent[axis_at] // parts).reshape([-1 if axis == axis_at else 1 for axis in range(len(extent))])
    return factor_of


def scatter_about(key, shape, width, bound, cuts=(), held_as=jnp.bfloat16):
    factor_of = shard_levels(key, shape, cuts, -0.22, 0.18) if cuts else 1.0
    drawn = jax.random.normal(key, shape, jnp.float32) * width * factor_of
    return jnp.minimum(jnp.maximum(drawn, -bound), bound).astype(held_as)


def setup_inputs(seed: int = 0) -> dict:
    seeds = jax.random.split(jax.random.key(seed), 4)
    return {
        "child_blocks": scatter_about(seeds[0], (CHILDREN * R, F), F ** -0.5, 0.0625, ((0, 8), (1, 4))),
        "sketch": scatter_about(seeds[1], (F, S), 1.0, 6.0, ((0, 4),)),
        "block_map": draw_block_map(jax.random.fold_in(seeds[3], 71), 0),
    }


def reference(child_blocks, sketch, block_map):
    panels = child_blocks.reshape(CHILDREN, R, F)

    def child_product(panel):
        return jnp.dot(panel.astype(jnp.float32), sketch.astype(jnp.float32), preferred_element_type=jnp.float32)
    sketch_rows = lax.map(child_product, panels)
    targets = jnp.arange(P_SIZE // BLK, dtype=jnp.int32)
    results = []
    for parent in range(PARENTS):
        extended = jnp.zeros((P_SIZE // BLK, BLK, S), jnp.float32)
        for sibling in range(SIBS):
            child = parent * SIBS + sibling
            one_hot = (block_map[child][:, None] == targets[None, :]).astype(jnp.float32)
            blocks = sketch_rows[child].reshape(R // BLK, BLK, S)
            extended = extended + jnp.einsum('bm,bks->mks', one_hot, blocks, precision=lax.Precision.HIGHEST)
        parent_sketch = extended.reshape(P_SIZE, S)
        gram = jnp.dot(parent_sketch.T, parent_sketch, precision=lax.Precision.HIGHEST)
        lower = jnp.linalg.cholesky(gram)
        results.append(jax.scipy.linalg.solve_triangular(lower, parent_sketch.T, lower=True))
    return jnp.concatenate(results, axis=1)
```

```python
import functools

import jax
import jax.numpy as jnp
from jax import lax
from jax.experimental import pallas as pl
from jax.experimental.pallas import tpu as pltpu
from jax.sharding import PartitionSpec as P

P_SIZE = 12288
BLK = 128
COLUMN_CHUNKS = 2
HIGHEST = lax.Precision.HIGHEST


def product_piece(panel, sketch, dest, sub, chunk, chunks):
    blocks, _, depth = panel.shape
    width = sketch.shape[1] // chunks
    step = 4 if blocks % 4 == 0 else 1

    def kernel(dest_ref, a_ref, b_ref, o_ref):
        rows = a_ref[...].reshape(step * sub, depth)
        o_ref[...] = jnp.dot(rows, b_ref[...], preferred_element_type=jnp.float32).reshape(step, sub, width)

    return pl.pallas_call(
        kernel,
        out_shape=jax.ShapeDtypeStruct((blocks, sub, width), jnp.float32),
        grid_spec=pltpu.PrefetchScalarGridSpec(
            num_scalar_prefetch=1,
            grid=(blocks // step,),
            in_specs=[
                pl.BlockSpec((step, sub, depth), lambda g, d: (g, d[0], 0)),
                pl.BlockSpec((depth, width), lambda g, d: (0, chunk)),
            ],
            out_specs=pl.BlockSpec((step, sub, width), lambda g, d: (g, 0, 0)),
        ),
        cost_estimate=pl.CostEstimate(
            flops=2 * blocks * sub * depth * width,
            bytes_accessed=2 * blocks * sub * depth + 2 * depth * width + 4 * blocks * sub * width,
            transcendentals=0,
        ),
        name="product_piece",
    )(dest.reshape(1), panel, sketch)


def pack_slots(held, inverse, slots):
    children = len(held)
    offsets = inverse.shape[1]
    _, sub, width = held[0].shape

    def kernel(inv_ref, *refs):
        for o in range(offsets):
            out = refs[children + o]

            def fill(j, carry, o=o, out=out):
                total = jnp.zeros((sub, width), jnp.float32)
                for k in range(children):
                    at = inv_ref[(k * offsets + o) * slots + j]
                    block = refs[k][jnp.maximum(at, 0)]
                    total = total + jnp.where(at >= 0, block, 0.0)
                out[j] = total
                return carry

            lax.fori_loop(0, slots, fill, 0)

    moved = 4 * sub * width * slots * offsets * (children + 1)
    return pl.pallas_call(
        kernel,
        out_shape=[jax.ShapeDtypeStruct((slots, sub, width), jnp.float32)] * offsets,
        in_specs=[pl.BlockSpec(memory_space=pltpu.SMEM)] + [pl.BlockSpec(memory_space=pltpu.VMEM)] * children,
        out_specs=[pl.BlockSpec(memory_space=pltpu.VMEM)] * offsets,
        cost_estimate=pl.CostEstimate(flops=moved, bytes_accessed=moved, transcendentals=0),
        name="pack_slots",
    )(inverse.reshape(-1), *held)


def gather_output(pieces, blk):
    cols, slots, sub, width = pieces.shape

    def kernel(x_ref, o_ref):
        o_ref[...] = x_ref[...].reshape(blk, width).T

    return pl.pallas_call(
        kernel,
        out_shape=jax.ShapeDtypeStruct((width, slots * blk), jnp.float32),
        grid=(slots,),
        in_specs=[pl.BlockSpec((cols, 1, sub, width), lambda j: (0, j, 0, 0))],
        out_specs=pl.BlockSpec((width, blk), lambda j: (0, j)),
        name="gather_output",
    )(pieces)


def shards(child_blocks, sketch, block_map):
    fronts, rows, cols = (lax.axis_size(a) for a in ("front", "row", "col"))
    siblings = min(4, fronts)
    front_here, row_here, col_here = (lax.axis_index(a) for a in ("front", "row", "col"))
    sib_here = front_here % siblings
    total_blocks = block_map.shape[1]
    blocks = total_blocks // rows
    sub = BLK // cols
    sketch_cols = sketch.shape[1]
    parent_blocks = P_SIZE // BLK
    slots = parent_blocks // (siblings * rows)
    spread = parent_blocks - total_blocks
    panel = child_blocks.reshape(blocks, BLK, child_blocks.shape[1])
    both = ("front", "row")

    def place(front, row):
        return front * rows + row

    def may_reach(row, sib, target_row):
        low, high = row * blocks, row * blocks + blocks - 1 + spread
        first = (sib * rows + target_row) * slots
        return low <= first + slots - 1 and first <= high

    maps = [block_map[0]]
    level = 1
    while level < siblings:
        pairs = [(i, i ^ level) for i in range(fronts)]
        maps = maps + [lax.ppermute(m, "front", pairs) for m in maps]
        level *= 2
    own = jnp.stack([lax.dynamic_slice_in_dim(m, row_here * blocks, blocks) for m in maps])
    offset_ids = jnp.arange(rows, dtype=jnp.int32)
    wanted = (sib_here * rows + (row_here ^ offset_ids))[:, None] * slots + jnp.arange(slots, dtype=jnp.int32)[None]
    hit = own[:, None, None, :] == wanted[None, :, :, None]
    inverse = jnp.max(jnp.where(hit, jnp.arange(blocks, dtype=jnp.int32), -1), axis=-1)

    def chunk_share(chunk):
        def piece(dest):
            return product_piece(panel, sketch, jnp.clip(dest, 0, cols - 1), sub, chunk, COLUMN_CHUNKS)

        came_up = came_down = None
        for stage in range(1, cols):
            up_dest, down_dest = cols - stage + col_here, stage - cols + col_here
            if stage <= cols // 2:
                up = down = piece(jnp.where(up_dest < cols, up_dest, down_dest))
            else:
                up, down = piece(up_dest), piece(down_dest)
            if came_up is not None:
                up, down = up + came_up, down + came_down
            came_up = lax.ppermute(up, "col", [(i, i + 1) for i in range(stage)])
            came_down = lax.ppermute(down, "col", [(i, i - 1) for i in range(cols - stage, cols)])
        mine = piece(col_here) + came_up + came_down
        held = [mine]
        level = 1
        while level < siblings:
            pairs = [(i, i ^ level) for i in range(fronts)]
            held = held + [lax.ppermute(h, "front", pairs) for h in held]
            level *= 2
        slotted = dict(enumerate(pack_slots(held, inverse, slots)))
        bits = [1 << k for k in range(rows.bit_length() - 1)]
        if chunk % 2:
            bits = bits[::-1]
        merged = [0]
        for bit in bits:
            kept = {}
            for o in sorted(slotted):
                if o & bit:
                    pairs = [
                        (place(f, r), place(f, r ^ bit))
                        for f in range(fronts)
                        for r in range(rows)
                        if any(may_reach(r ^ m, f % siblings, r ^ o) for m in merged)
                    ]
                    kept[o ^ bit] = slotted[o ^ bit] + lax.ppermute(slotted[o], both, pairs)
            slotted = kept
            merged = merged + [m | bit for m in merged]
        return slotted[0].reshape(slots * sub, sketch_cols // COLUMN_CHUNKS)

    share = jnp.concatenate([chunk_share(h) for h in range(COLUMN_CHUNKS)], axis=1)
    gram = lax.dot_general(share, share, (((0,), (0,)), ((), ())), precision=HIGHEST)

    steps = []
    level = 1
    while level < siblings:
        steps.append(("front", level, fronts, front_here))
        level *= 2
    for name, size, here in (("row", rows, row_here), ("col", cols, col_here)):
        level = 1
        while level < size:
            steps.append((name, level, size, here))
            level *= 2
    part = gram
    for name, level, size, here in steps:
        half = part.shape[0] // 2
        upper = (here & level) != 0
        low, high = part[:half], part[half:]
        sent = lax.ppermute(jnp.where(upper, low, high), name, [(i, i ^ level) for i in range(size)])
        part = jnp.where(upper, high, low) + sent
    for name, level, size, here in steps[::-1]:
        upper = (here & level) != 0
        other = lax.ppermute(part, name, [(i, i ^ level) for i in range(size)])
        part = jnp.concatenate([jnp.where(upper, other, part), jnp.where(upper, part, other)], axis=0)
    gram = part

    lower = jnp.linalg.cholesky(gram)
    inverse_lower = jax.scipy.linalg.solve_triangular(lower, jnp.eye(sketch_cols, dtype=jnp.float32), lower=True)
    basis = lax.dot_general(share, inverse_lower, (((1,), (1,)), ((), ())), precision=HIGHEST)
    width = sketch_cols // cols
    basis = basis.reshape(slots * sub, cols, width).transpose(1, 0, 2)
    basis = lax.all_to_all(basis, "col", 0, 0, tiled=True)
    return gather_output(basis.reshape(cols, slots, sub, width), BLK)


def solution(mesh):
    placed = (P(("front", "row"), "col"), P("col", None), P("front", None))
    return jax.shard_map(
        shards, mesh=mesh, in_specs=placed, out_specs=P("col", ("front", "row")), check_vma=False
    )
```

```python
import jax
import jax.numpy as jnp
from jax import lax
from jax.experimental import pallas as pl
from jax.experimental.pallas import tpu as pltpu
from jax.sharding import PartitionSpec as P

P_SIZE = 12288
BLK = 128
COLUMN_CHUNKS = 2


def product_pieces(panel, sketch, dests, sub, chunks):
    blocks, _, depth = panel.shape
    count = len(dests)
    width = sketch.shape[1] // chunks
    step = max(blocks // 2, 1)

    def kernel(dest_ref, a_ref, b_ref, *outs):
        product = jnp.dot(a_ref[...].reshape(step * sub, depth), b_ref[...], preferred_element_type=jnp.float32)
        rows = pl.ds(pl.program_id(1) * step, step)
        for k in range(count):

            @pl.when(pl.program_id(0) == k)
            def _():
                for h in range(chunks):
                    outs[k * chunks + h][rows] = product[:, h * width : (h + 1) * width].reshape(step, sub, width)

    outs = pl.pallas_call(
        kernel,
        out_shape=[jax.ShapeDtypeStruct((blocks, sub, width), jnp.float32)] * (count * chunks),
        grid_spec=pltpu.PrefetchScalarGridSpec(
            num_scalar_prefetch=1,
            grid=(count, blocks // step),
            in_specs=[
                pl.BlockSpec((step, sub, depth), lambda p, g, d: (g, d[p], 0)),
                pl.BlockSpec(memory_space=pltpu.VMEM),
            ],
            out_specs=[pl.BlockSpec(memory_space=pltpu.VMEM)] * (count * chunks),
        ),
        cost_estimate=pl.CostEstimate(
            flops=2 * count * blocks * sub * depth * width * chunks,
            bytes_accessed=count * blocks * sub * (2 * depth + 4 * width * chunks) + 2 * depth * width * chunks,
            transcendentals=0,
        ),
        name="product_pieces",
    )(jnp.stack(dests), panel, sketch)
    return [outs[k * chunks : (k + 1) * chunks] for k in range(count)]


def pack_slots(held, inverse, slots):
    children = len(held)
    offsets = inverse.shape[1]
    _, sub, width = held[0].shape

    def kernel(inv_ref, *refs):
        for o in range(offsets):
            out = refs[children + o]

            def fill(j, carry, o=o, out=out):
                total = jnp.zeros((sub, width), jnp.float32)
                for k in range(children):
                    at = inv_ref[(k * offsets + o) * slots + j]
                    block = refs[k][jnp.maximum(at, 0)]
                    total = total + jnp.where(at >= 0, block, 0.0)
                out[j] = total
                return carry

            lax.fori_loop(0, slots, fill, 0)

    moved = 4 * sub * width * slots * offsets * (children + 1)
    return pl.pallas_call(
        kernel,
        out_shape=[jax.ShapeDtypeStruct((slots, sub, width), jnp.float32)] * offsets,
        in_specs=[pl.BlockSpec(memory_space=pltpu.SMEM)] + [pl.BlockSpec(memory_space=pltpu.VMEM)] * children,
        out_specs=[pl.BlockSpec(memory_space=pltpu.VMEM)] * offsets,
        cost_estimate=pl.CostEstimate(flops=moved, bytes_accessed=moved, transcendentals=0),
        name="pack_slots",
    )(inverse.reshape(-1), *held)


def on_last(a, b):
    return lax.dot_general(a, b, (((1,), (1,)), ((), ())), preferred_element_type=jnp.float32)


def on_first(a, b):
    return lax.dot_general(a, b, (((0,), (0,)), ((), ())), preferred_element_type=jnp.float32)


def plain(a, b):
    return jnp.dot(a, b, preferred_element_type=jnp.float32)


def split(x):
    high = x.astype(jnp.bfloat16)
    return high, (x - high.astype(jnp.float32)).astype(jnp.bfloat16)


def triple(dot, a, b):
    return dot(a[0], b[0]) + (dot(a[0], b[1]) + dot(a[1], b[0]))


def packed_gram(parts, tile):
    rows = parts[0].shape[0]
    total = sum(p.shape[1] for p in parts)
    count = total // tile

    def kernel(*refs):
        high, low = split(jnp.concatenate([r[...] for r in refs[:-1]], axis=1))
        at = 0
        for i in range(count):
            here, upto = slice(i * tile, (i + 1) * tile), slice(0, (i + 1) * tile)
            strip = triple(on_first, (high[:, here], low[:, here]), (high[:, upto], low[:, upto]))
            for j in range(i + 1):
                refs[-1][at * tile : (at + 1) * tile, :] = strip[:, j * tile : (j + 1) * tile]
                at += 1

    blocks = count * (count + 1) // 2
    return pl.pallas_call(
        kernel,
        out_shape=jax.ShapeDtypeStruct((blocks * tile, tile), jnp.float32),
        in_specs=[pl.BlockSpec(memory_space=pltpu.VMEM)] * len(parts),
        out_specs=pl.BlockSpec(memory_space=pltpu.VMEM),
        cost_estimate=pl.CostEstimate(
            flops=6 * blocks * tile * tile * rows,
            bytes_accessed=4 * (rows * total + blocks * tile * tile),
            transcendentals=0,
        ),
        name="packed_gram",
    )(*parts)


def basis_pieces(packed, parts, tile):
    rows = parts[0].shape[0]
    n = sum(p.shape[1] for p in parts)
    count = n // tile
    small, enough = 1e-2, 4e-4

    def kernel(packed_ref, *refs):
        share_refs, (out_ref, g_ref, x_ref, e_ref) = refs[: len(parts)], refs[len(parts) :]
        at = 0
        for i in range(count):
            here = slice(i * tile, (i + 1) * tile)
            for j in range(i + 1):
                there = slice(j * tile, (j + 1) * tile)
                block = packed_ref[at * tile : (at + 1) * tile, :]
                g_ref[here, there] = block
                if j < i:
                    g_ref[there, here] = block.T
                at += 1
        row_id = lax.broadcasted_iota(jnp.int32, (n, n), 0)
        col_id = lax.broadcasted_iota(jnp.int32, (n, n), 1)

        def eye():
            return jnp.where(row_id == col_id, 1.0, 0.0)

        def half_lower(e):
            return jnp.where(row_id > col_id, e, jnp.where(row_id == col_id, 0.5 * e, 0.0))

        g = g_ref[...]
        diagonal = jnp.where(row_id == col_id, g, 0.0)
        down = 1.0 / jnp.sqrt(jnp.sum(diagonal, axis=1, keepdims=True))
        across = 1.0 / jnp.sqrt(jnp.sum(diagonal, axis=0, keepdims=True))
        x_ref[...] = jnp.where(row_id == col_id, down, 0.0)
        start = g * down * across - eye()
        e_ref[...] = start

        def rough(state):
            e = e_ref[...]
            f = half_lower(e)
            fb, eb = f.astype(jnp.bfloat16), e.astype(jnp.bfloat16)
            t = plain(fb, eb)
            e = on_last((f + t).astype(jnp.bfloat16), fb) - t - on_last(eb, fb)
            e_ref[...] = e
            x = x_ref[...]
            x_ref[...] = x - plain(fb, x.astype(jnp.bfloat16))
            return state[0] + 1, jnp.sum(e * e)

        lax.while_loop(lambda s: (s[0] < 12) & (s[1] > small) & (s[1] < 1e6), rough, (0, jnp.sum(start * start)))

        def fine(state):
            x = split(x_ref[...])
            e = triple(on_last, split(triple(plain, x, split(g_ref[...]))), x) - eye()
            x_ref[...] = x_ref[...] - plain(half_lower(e).astype(jnp.bfloat16), x[0])
            return state[0] + 1, jnp.sum(e * e)

        _, last = lax.while_loop(
            lambda s: (s[0] < 4) & jnp.logical_not(s[1] < enough), fine, (0, jnp.float32(1.0))
        )

        @pl.when(jnp.logical_not(last < enough))
        def _():
            x_ref[...] = eye()
            e_ref[...] = g_ref[...]
            lane = lax.broadcasted_iota(jnp.int32, (1, n), 1)
            below = lax.broadcasted_iota(jnp.int32, (n, 1), 0)

            def eliminate(j, carry):
                row = e_ref[pl.ds(j, 1), :]
                scale = 1.0 / jnp.sqrt(jnp.sum(jnp.where(lane == j, row, 0.0), axis=1, keepdims=True))
                row = jnp.where(lane > j, row * scale, 0.0)
                solved = x_ref[pl.ds(j, 1), :] * scale
                column = jnp.sum(jnp.where(col_id == j, e_ref[...], 0.0), axis=1, keepdims=True) * scale
                column = jnp.where(below > j, column, 0.0)
                e_ref[...] = e_ref[...] - column * row
                x_ref[...] = x_ref[...] - column * solved
                x_ref[pl.ds(j, 1), :] = solved
                return carry

            lax.fori_loop(0, n, eliminate, 0)

        share = split(jnp.concatenate([r[...] for r in share_refs], axis=1))
        for i in range(count):
            upto = (i + 1) * tile
            x = split(x_ref[i * tile : upto, :upto])
            out_ref[i] = triple(on_last, (share[0][:, :upto], share[1][:, :upto]), x)

    return pl.pallas_call(
        kernel,
        out_shape=jax.ShapeDtypeStruct((count, rows, tile), jnp.float32),
        in_specs=[pl.BlockSpec(memory_space=pltpu.VMEM)] * (1 + len(parts)),
        out_specs=pl.BlockSpec(memory_space=pltpu.VMEM),
        scratch_shapes=[pltpu.VMEM((n, n), jnp.float32)] * 3,
        cost_estimate=pl.CostEstimate(flops=12 * n * n * n, bytes_accessed=4 * n * (n + rows), transcendentals=0),
        name="basis_pieces",
    )(packed, *parts)


def lay_out(pieces, here, slots, sub, blk):
    width = pieces[0].shape[1]

    def kernel(here_ref, *refs):
        out_ref, block_ref = refs[-2:]
        for j in range(slots):
            for k in range(len(pieces)):
                spot = pl.ds(pl.multiple_of((here_ref[0] ^ k) * sub, sub), sub)
                block_ref[j, spot, :] = refs[k][j * sub : (j + 1) * sub, :]
        for j in range(slots):
            out_ref[:, j * blk : (j + 1) * blk] = block_ref[j].T

    return pl.pallas_call(
        kernel,
        out_shape=jax.ShapeDtypeStruct((width, slots * blk), jnp.float32),
        in_specs=[pl.BlockSpec(memory_space=pltpu.SMEM)] + [pl.BlockSpec(memory_space=pltpu.VMEM)] * len(pieces),
        out_specs=pl.BlockSpec(memory_space=pltpu.VMEM),
        scratch_shapes=[pltpu.VMEM((slots, blk, width), jnp.float32)],
        name="lay_out",
    )(here.reshape(1), *pieces)


def shards(child_blocks, sketch, block_map):
    fronts, rows, cols = (lax.axis_size(a) for a in ("front", "row", "col"))
    siblings = min(4, fronts)
    front_here, row_here, col_here = (lax.axis_index(a) for a in ("front", "row", "col"))
    sib_here = front_here % siblings
    total_blocks = block_map.shape[1]
    blocks = total_blocks // rows
    sub = BLK // cols
    sketch_cols = sketch.shape[1]
    parent_blocks = P_SIZE // BLK
    slots = parent_blocks // (siblings * rows)
    spread = parent_blocks - total_blocks
    panel = child_blocks.reshape(blocks, BLK, child_blocks.shape[1])
    both = ("front", "row")

    def place(front, row):
        return front * rows + row

    def may_reach(row, sib, target_row):
        low, high = row * blocks, row * blocks + blocks - 1 + spread
        first = (sib * rows + target_row) * slots
        return low <= first + slots - 1 and first <= high

    maps = [block_map[0]]
    level = 1
    while level < siblings:
        pairs = [(i, i ^ level) for i in range(fronts)]
        maps = maps + [lax.ppermute(m, "front", pairs) for m in maps]
        level *= 2
    own = jnp.stack([lax.dynamic_slice_in_dim(m, row_here * blocks, blocks) for m in maps])
    offset_ids = jnp.arange(rows, dtype=jnp.int32)
    wanted = (sib_here * rows + (row_here ^ offset_ids))[:, None] * slots + jnp.arange(slots, dtype=jnp.int32)[None]
    hit = own[:, None, None, :] == wanted[None, :, :, None]
    inverse = jnp.max(jnp.where(hit, jnp.arange(blocks, dtype=jnp.int32), -1), axis=-1)

    def clipped(dest):
        return jnp.clip(dest, 0, cols - 1)

    wants = []
    for stage in range(1, cols):
        up_dest, down_dest = cols - stage + col_here, stage - cols + col_here
        if stage <= cols // 2:
            wants.append(clipped(jnp.where(up_dest < cols, up_dest, down_dest)))
        else:
            wants += [clipped(up_dest), clipped(down_dest)]
    wants.append(col_here)
    products = product_pieces(panel, sketch, wants[:1], sub, COLUMN_CHUNKS)
    products += product_pieces(panel, sketch, wants[1:], sub, COLUMN_CHUNKS)

    def chunk_share(chunk):
        pieces = iter(products)
        came_up = came_down = None
        for stage in range(1, cols):
            up = down = next(pieces)[chunk]
            if stage > cols // 2:
                down = next(pieces)[chunk]
            if came_up is not None:
                up, down = up + came_up, down + came_down
            came_up = lax.ppermute(up, "col", [(i, i + 1) for i in range(stage)])
            came_down = lax.ppermute(down, "col", [(i, i - 1) for i in range(cols - stage, cols)])
        mine = next(pieces)[chunk] + came_up + came_down
        held = [mine]
        level = 1
        while level < siblings:
            pairs = [(i, i ^ level) for i in range(fronts)]
            held = held + [lax.ppermute(h, "front", pairs) for h in held]
            level *= 2
        slotted = dict(enumerate(pack_slots(held, inverse, slots)))
        bits = [1 << k for k in range(rows.bit_length() - 1)]
        if chunk % 2:
            bits = bits[::-1]
        merged = [0]
        for bit in bits:
            kept = {}
            for o in sorted(slotted):
                if o & bit:
                    pairs = [
                        (place(f, r), place(f, r ^ bit))
                        for f in range(fronts)
                        for r in range(rows)
                        if any(may_reach(r ^ m, f % siblings, r ^ o) for m in merged)
                    ]
                    kept[o ^ bit] = slotted[o ^ bit] + lax.ppermute(slotted[o], both, pairs)
            slotted = kept
            merged = merged + [m | bit for m in merged]
        return slotted[0].reshape(slots * sub, sketch_cols // COLUMN_CHUNKS)

    width = sketch_cols // cols
    shares = [chunk_share(h) for h in range(COLUMN_CHUNKS)]
    packed = packed_gram(shares, width)

    def swap(x, name, level):
        return lax.ppermute(x, name, [(i, i ^ level) for i in range(lax.axis_size(name))])

    levels = [1 << k for k in range(siblings.bit_length() - 1)]
    for level in levels:
        half = packed.shape[0] // 2
        upper = (sib_here & level) != 0
        low, high = packed[:half], packed[half:]
        packed = jnp.where(upper, high, low) + swap(jnp.where(upper, low, high), "front", level)
    parts = packed.reshape(rows, packed.shape[0] // rows, width)

    def part_of(row):
        return lax.dynamic_index_in_dim(parts, row, 0, keepdims=False)

    packed = part_of(row_here)
    for k in list(range(1, rows))[::-1]:
        packed = packed + swap(part_of(row_here ^ k), "row", k)
    packed = packed + sum(swap(packed, "col", k) for k in list(range(1, cols))[::-1])
    parts = jnp.stack([packed] + [swap(packed, "row", k) for k in range(1, rows)])
    packed = jnp.concatenate([part_of(row_here ^ k) for k in range(rows)], axis=0)
    for level in levels[::-1]:
        upper = (sib_here & level) != 0
        other = swap(packed, "front", level)
        packed = jnp.concatenate([jnp.where(upper, other, packed), jnp.where(upper, packed, other)], axis=0)

    basis = basis_pieces(packed, shares, width)
    pieces = [lax.dynamic_index_in_dim(basis, col_here, 0, keepdims=False)]
    for k in range(1, cols):
        pieces.append(swap(lax.dynamic_index_in_dim(basis, col_here ^ k, 0, keepdims=False), "col", k))
    return lay_out(pieces, col_here, slots, sub, BLK)


def solution(mesh):
    placed = (P(("front", "row"), "col"), P("col", None), P("front", None))
    return jax.shard_map(
        shards, mesh=mesh, in_specs=placed, out_specs=P("col", ("front", "row")), check_vma=False
    )
```

```python
import jax
import jax.numpy as jnp
from jax import lax
from jax.experimental import pallas as pl
from jax.experimental.pallas import tpu as pltpu
from jax.sharding import PartitionSpec as P


P_SIZE = 12288
BLK = 128
COLUMN_CHUNKS = 2


def grant(mebibytes):
    return pltpu.CompilerParams(vmem_limit_bytes=mebibytes << 20)


def product_pieces(panel, sketch, dests, sub, chunks):
    blocks, _, depth = panel.shape
    count = len(dests)
    width = sketch.shape[1] // chunks
    step = max(blocks // 2, 1)

    def kernel(dest_ref, a_ref, b_ref, *outs):
        product = jnp.dot(a_ref[...].reshape(step * sub, depth), b_ref[...], preferred_element_type=jnp.float32)
        rows = pl.ds(pl.program_id(1) * step, step)
        for k in range(count):

            @pl.when(pl.program_id(0) == k)
            def _():
                for h in range(chunks):
                    outs[k * chunks + h][rows] = product[:, h * width : (h + 1) * width].reshape(step, sub, width)

    outs = pl.pallas_call(
        kernel,
        out_shape=[jax.ShapeDtypeStruct((blocks, sub, width), jnp.float32)] * (count * chunks),
        grid_spec=pltpu.PrefetchScalarGridSpec(
            num_scalar_prefetch=1,
            grid=(count, blocks // step),
            in_specs=[
                pl.BlockSpec((step, sub, depth), lambda p, g, d: (g, d[p], 0)),
                pl.BlockSpec(memory_space=pltpu.VMEM),
            ],
            out_specs=[pl.BlockSpec(memory_space=pltpu.VMEM)] * (count * chunks),
        ),
        cost_estimate=pl.CostEstimate(
            flops=2 * count * blocks * sub * depth * width * chunks,
            bytes_accessed=count * blocks * sub * (2 * depth + 4 * width * chunks) + 2 * depth * width * chunks,
            transcendentals=0,
        ),
        compiler_params=grant(28),
        name="product_pieces",
    )(jnp.stack(dests), panel, sketch)
    return [outs[k * chunks : (k + 1) * chunks] for k in range(count)]


def pack_slots(held, inverse, slots):
    children = len(held)
    offsets = inverse.shape[1]
    _, sub, width = held[0].shape

    def kernel(inv_ref, *refs):
        for o in range(offsets):
            out = refs[children + o]

            def fill(j, carry, o=o, out=out):
                total = jnp.zeros((sub, width), jnp.float32)
                for k in range(children):
                    at = inv_ref[(k * offsets + o) * slots + j]
                    block = refs[k][jnp.maximum(at, 0)]
                    total = total + jnp.where(at >= 0, block, 0.0)
                out[j] = total
                return carry

            lax.fori_loop(0, slots, fill, 0)

    moved = 4 * sub * width * slots * offsets * (children + 1)
    return pl.pallas_call(
        kernel,
        out_shape=[jax.ShapeDtypeStruct((slots, sub, width), jnp.float32)] * offsets,
        in_specs=[pl.BlockSpec(memory_space=pltpu.SMEM)] + [pl.BlockSpec(memory_space=pltpu.VMEM)] * children,
        out_specs=[pl.BlockSpec(memory_space=pltpu.VMEM)] * offsets,
        cost_estimate=pl.CostEstimate(flops=moved, bytes_accessed=moved, transcendentals=0),
        compiler_params=grant(12),
        name="pack_slots",
    )(inverse.reshape(-1), *held)


def on_last(a, b):
    return lax.dot_general(a, b, (((1,), (1,)), ((), ())), preferred_element_type=jnp.float32)


def on_first(a, b):
    return lax.dot_general(a, b, (((0,), (0,)), ((), ())), preferred_element_type=jnp.float32)


def plain(a, b):
    return jnp.dot(a, b, preferred_element_type=jnp.float32)


def split(x):
    high = x.astype(jnp.bfloat16)
    return high, (x - high.astype(jnp.float32)).astype(jnp.bfloat16)


def triple(dot, a, b):
    return dot(a[0], b[0]) + (dot(a[0], b[1]) + dot(a[1], b[0]))


def gram_pieces(arrived, here, siblings, members, tile):
    slots, sub, width = arrived[0][0].shape
    rows, n = slots * sub, width * len(arrived)
    count = n // tile
    height = count * (count + 1) // 2 * tile
    piece = height // (siblings * members)
    counts = [len(a) for a in arrived]

    def kernel(here_ref, *refs):
        inputs, (share_ref, *out_refs, packed_ref) = refs[: sum(counts)], refs[sum(counts) :]
        at = 0
        for h, addends in enumerate(counts):
            share_ref[:, h * width : (h + 1) * width] = sum(r[...] for r in inputs[at : at + addends]).reshape(rows, width)
            at += addends
        high, low = split(share_ref[...])
        at = 0
        for i in range(count):
            here, upto = slice(i * tile, (i + 1) * tile), slice(0, (i + 1) * tile)
            strip = triple(on_first, (high[:, here], low[:, here]), (high[:, upto], low[:, upto]))
            for j in range(i + 1):
                packed_ref[at * tile : (at + 1) * tile, :] = strip[:, j * tile : (j + 1) * tile]
                at += 1
        for s in range(siblings):
            for m in range(members):
                spot = ((here_ref[0] ^ s) * members + (here_ref[1] ^ m)) * piece
                out_refs[s][m * piece : (m + 1) * piece, :] = packed_ref[pl.ds(pl.multiple_of(spot, 8), piece), :]

    flat = [x for a in arrived for x in a]
    outs = pl.pallas_call(
        kernel,
        out_shape=[jax.ShapeDtypeStruct((rows, n), jnp.float32)]
        + [jax.ShapeDtypeStruct((members * piece, tile), jnp.float32)] * siblings,
        in_specs=[pl.BlockSpec(memory_space=pltpu.SMEM)] + [pl.BlockSpec(memory_space=pltpu.VMEM)] * len(flat),
        out_specs=[pl.BlockSpec(memory_space=pltpu.VMEM)] * (1 + siblings),
        scratch_shapes=[pltpu.VMEM((height, tile), jnp.float32)],
        cost_estimate=pl.CostEstimate(
            flops=6 * height * tile * rows, bytes_accessed=4 * (len(flat) + 1) * rows * width, transcendentals=0
        ),
        compiler_params=grant(20),
        name="gram_pieces",
    )(here, *flat)
    return outs[0], list(outs[1:])


def basis_pieces(pieces, share, here, siblings, tile):
    rows, n = share.shape
    count = n // tile
    members = len(pieces)
    height = count * (count + 1) // 2 * tile
    piece = height // (siblings * members)
    small, enough = 1e-2, 4e-4

    def kernel(here_ref, *refs):
        piece_refs, share_ref = refs[:members], refs[members]
        out_refs, (packed_ref, g_ref, x_ref, e_ref) = refs[members + 1 : -4], refs[-4:]
        for s in range(siblings):
            for m in range(members):
                spot = ((here_ref[0] ^ s) * members + (here_ref[1] ^ m)) * piece
                packed_ref[pl.ds(pl.multiple_of(spot, 8), piece), :] = piece_refs[m][s * piece : (s + 1) * piece, :]
        at = 0
        for i in range(count):
            here = slice(i * tile, (i + 1) * tile)
            for j in range(i + 1):
                there = slice(j * tile, (j + 1) * tile)
                block = packed_ref[at * tile : (at + 1) * tile, :]
                g_ref[here, there] = block
                if j < i:
                    g_ref[there, here] = block.T
                at += 1
        row_id = lax.broadcasted_iota(jnp.int32, (n, n), 0)
        col_id = lax.broadcasted_iota(jnp.int32, (n, n), 1)

        def eye():
            return jnp.where(row_id == col_id, 1.0, 0.0)

        def half_lower(e):
            return jnp.where(row_id > col_id, e, jnp.where(row_id == col_id, 0.5 * e, 0.0))

        g = g_ref[...]
        diagonal = jnp.where(row_id == col_id, g, 0.0)
        down = 1.0 / jnp.sqrt(jnp.sum(diagonal, axis=1, keepdims=True))
        across = 1.0 / jnp.sqrt(jnp.sum(diagonal, axis=0, keepdims=True))
        x_ref[...] = jnp.where(row_id == col_id, down, 0.0)
        start = g * down * across - eye()
        e_ref[...] = start

        def rough(state):
            e = e_ref[...]
            f = half_lower(e)
            fb, eb = f.astype(jnp.bfloat16), e.astype(jnp.bfloat16)
            t = plain(fb, eb)
            e = on_last((f + t).astype(jnp.bfloat16), fb) - t - on_last(eb, fb)
            e_ref[...] = e
            x = x_ref[...]
            x_ref[...] = x - plain(fb, x.astype(jnp.bfloat16))
            return state[0] + 1, jnp.sum(e * e)

        lax.while_loop(lambda s: (s[0] < 12) & (s[1] > small) & (s[1] < 1e6), rough, (0, jnp.sum(start * start)))

        def fine(state):
            x = split(x_ref[...])
            e = triple(on_last, split(triple(plain, x, split(g_ref[...]))), x) - eye()
            x_ref[...] = x_ref[...] - plain(half_lower(e).astype(jnp.bfloat16), x[0])
            return state[0] + 1, jnp.sum(e * e)

        _, last = lax.while_loop(
            lambda s: (s[0] < 4) & jnp.logical_not(s[1] < enough), fine, (0, jnp.float32(1.0))
        )

        @pl.when(jnp.logical_not(last < enough))
        def _():
            x_ref[...] = eye()
            e_ref[...] = g_ref[...]
            lane = lax.broadcasted_iota(jnp.int32, (1, n), 1)
            below = lax.broadcasted_iota(jnp.int32, (n, 1), 0)

            def eliminate(j, carry):
                row = e_ref[pl.ds(j, 1), :]
                scale = 1.0 / jnp.sqrt(jnp.sum(jnp.where(lane == j, row, 0.0), axis=1, keepdims=True))
                row = jnp.where(lane > j, row * scale, 0.0)
                solved = x_ref[pl.ds(j, 1), :] * scale
                column = jnp.sum(jnp.where(col_id == j, e_ref[...], 0.0), axis=1, keepdims=True) * scale
                column = jnp.where(below > j, column, 0.0)
                e_ref[...] = e_ref[...] - column * row
                x_ref[...] = x_ref[...] - column * solved
                x_ref[pl.ds(j, 1), :] = solved
                return carry

            lax.fori_loop(0, n, eliminate, 0)

        split_share = split(share_ref[...])
        for k in range(count):
            strip = pl.multiple_of((here_ref[2] ^ k) * tile, tile)
            out_refs[k][...] = triple(on_last, split_share, split(x_ref[pl.ds(strip, tile), :]))

    return pl.pallas_call(
        kernel,
        out_shape=[jax.ShapeDtypeStruct((rows, tile), jnp.float32)] * count,
        in_specs=[pl.BlockSpec(memory_space=pltpu.SMEM)] + [pl.BlockSpec(memory_space=pltpu.VMEM)] * (1 + members),
        out_specs=[pl.BlockSpec(memory_space=pltpu.VMEM)] * count,
        scratch_shapes=[pltpu.VMEM((height, tile), jnp.float32)] + [pltpu.VMEM((n, n), jnp.float32)] * 3,
        cost_estimate=pl.CostEstimate(flops=12 * n * n * n, bytes_accessed=4 * n * (n + rows), transcendentals=0),
        compiler_params=grant(40),
        name="basis_pieces",
    )(here, *pieces, share)


def lay_out(pieces, here, slots, sub, blk):
    width = pieces[0].shape[1]

    def kernel(here_ref, *refs):
        out_ref, block_ref = refs[-2:]
        for j in range(slots):
            for k in range(len(pieces)):
                spot = pl.ds(pl.multiple_of((here_ref[0] ^ k) * sub, sub), sub)
                block_ref[j, spot, :] = refs[k][j * sub : (j + 1) * sub, :]
        for j in range(slots):
            out_ref[:, j * blk : (j + 1) * blk] = block_ref[j].T

    return pl.pallas_call(
        kernel,
        out_shape=jax.ShapeDtypeStruct((width, slots * blk), jnp.float32),
        in_specs=[pl.BlockSpec(memory_space=pltpu.SMEM)] + [pl.BlockSpec(memory_space=pltpu.VMEM)] * len(pieces),
        out_specs=pl.BlockSpec(memory_space=pltpu.VMEM),
        scratch_shapes=[pltpu.VMEM((slots, blk, width), jnp.float32)],
        compiler_params=grant(12),
        name="lay_out",
    )(here.reshape(1), *pieces)


def shards(child_blocks, sketch, block_map):
    fronts, rows, cols = (lax.axis_size(a) for a in ("front", "row", "col"))
    siblings = min(4, fronts)
    front_here, row_here, col_here = (lax.axis_index(a) for a in ("front", "row", "col"))
    sib_here = front_here % siblings
    total_blocks = block_map.shape[1]
    blocks = total_blocks // rows
    sub = BLK // cols
    sketch_cols = sketch.shape[1]
    parent_blocks = P_SIZE // BLK
    slots = parent_blocks // (siblings * rows)
    spread = parent_blocks - total_blocks
    panel = child_blocks.reshape(blocks, BLK, child_blocks.shape[1])
    both = ("front", "row")

    def place(front, row):
        return front * rows + row

    def may_reach(row, sib, target_row):
        low, high = row * blocks, row * blocks + blocks - 1 + spread
        first = (sib * rows + target_row) * slots
        return low <= first + slots - 1 and first <= high

    maps = [block_map[0]]
    level = 1
    while level < siblings:
        pairs = [(i, i ^ level) for i in range(fronts)]
        maps = maps + [lax.ppermute(m, "front", pairs) for m in maps]
        level *= 2
    own = jnp.stack([lax.dynamic_slice_in_dim(m, row_here * blocks, blocks) for m in maps])
    offset_ids = jnp.arange(rows, dtype=jnp.int32)
    wanted = (sib_here * rows + (row_here ^ offset_ids))[:, None] * slots + jnp.arange(slots, dtype=jnp.int32)[None]
    hit = own[:, None, None, :] == wanted[None, :, :, None]
    inverse = jnp.max(jnp.where(hit, jnp.arange(blocks, dtype=jnp.int32), -1), axis=-1)

    def clipped(dest):
        return jnp.clip(dest, 0, cols - 1)

    wants = []
    for stage in range(1, cols):
        up_dest, down_dest = cols - stage + col_here, stage - cols + col_here
        if stage <= cols // 2:
            wants.append(clipped(jnp.where(up_dest < cols, up_dest, down_dest)))
        else:
            wants += [clipped(up_dest), clipped(down_dest)]
    wants.append(col_here)
    panel = pltpu.with_memory_space_constraint(panel, pltpu.HBM)
    products = [*product_pieces(panel, sketch, wants[:1], sub, COLUMN_CHUNKS)]
    products += product_pieces(panel, sketch, wants[1:], sub, COLUMN_CHUNKS)

    arrived = []
    for chunk in range(COLUMN_CHUNKS):
        pieces = iter(products)
        came_up = came_down = None
        for stage in range(1, cols):
            up = down = next(pieces)[chunk]
            if stage > cols // 2:
                down = next(pieces)[chunk]
            if came_up is not None:
                up, down = up + came_up, down + came_down
            came_up = lax.ppermute(up, "col", [(i, i + 1) for i in range(stage)])
            came_down = lax.ppermute(down, "col", [(i, i - 1) for i in range(cols - stage, cols)])
        held = [next(pieces)[chunk] + came_up + came_down]
        level = 1
        while level < siblings:
            pairs = [(i, i ^ level) for i in range(fronts)]
            held = held + [lax.ppermute(h, "front", pairs) for h in held]
            level *= 2
        slotted = pack_slots(held, inverse, slots)
        came = [slotted[0]]
        for k in range(1, rows)[::-1]:
            pairs = [
                (place(f, r), place(f, r ^ k))
                for f in range(fronts)
                for r in range(rows)
                if may_reach(r, f % siblings, r ^ k)
            ]
            came.append(lax.ppermute(slotted[k], both, pairs))
        arrived.append(came)

    width = sketch_cols // cols
    here = jnp.stack([sib_here, row_here, col_here])
    share, halves = gram_pieces(arrived, here, siblings, rows, width)

    def swap(x, name, level):
        return lax.ppermute(x, name, [(i, i ^ level) for i in range(lax.axis_size(name))])

    levels = [1 << k for k in range(siblings.bit_length() - 1)]
    kept = dict(enumerate(halves))
    for level in levels:
        kept = {s: kept[s] + swap(kept[s ^ level], "front", level) for s in kept if not s & level}
    parts = kept[0].reshape(rows, kept[0].shape[0] // rows, width)
    piece = parts[0]
    for k in range(1, rows)[::-1]:
        piece = piece + swap(parts[k], "row", k)
    piece = piece + sum(swap(piece, "col", k) for k in range(1, cols)[::-1])
    mine = [piece]
    for level in levels:
        mine = mine + [swap(p, "front", level) for p in mine]
    mine = jnp.concatenate(mine, axis=0)
    pieces = [mine] + [swap(mine, "row", k) for k in range(1, rows)]

    basis = basis_pieces(pieces, share, here, siblings, width)
    pieces = [basis[0]] + [swap(basis[k], "col", k) for k in range(1, cols)]
    return lay_out(pieces, col_here, slots, sub, BLK)


def solution(mesh):
    placed = (P(("front", "row"), "col"), P("col", None), P("front", None))

    return jax.shard_map(shards, mesh=mesh, in_specs=placed, out_specs=P("col", ("front", "row")), check_vma=False)
```

```python
import jax
import jax.numpy as jnp
from jax import lax
from jax.experimental import pallas as pl
from jax.experimental.pallas import tpu as pltpu
from jax.sharding import PartitionSpec as P


P_SIZE = 12288
BLK = 128
COLUMN_CHUNKS = 2


def grant(mebibytes):
    return pltpu.CompilerParams(vmem_limit_bytes=mebibytes << 20)


def product_pieces(panel, sketch, dests, sub, chunks, chunk=None):
    blocks, _, depth = panel.shape
    count = len(dests)
    outs_each = chunks if chunk is None else 1
    width = sketch.shape[1] // chunks
    across = width * outs_each
    step = max(blocks // 2, 1) if chunk is None else max(blocks // 4, 1)

    def kernel(dest_ref, a_ref, b_ref, *outs):
        product = jnp.dot(a_ref[...].reshape(step * sub, depth), b_ref[...], preferred_element_type=jnp.float32)
        rows = pl.ds(pl.program_id(1) * step, step)
        for k in range(count):

            @pl.when(pl.program_id(0) == k)
            def _():
                for h in range(outs_each):
                    part = product[:, h * width : (h + 1) * width]
                    outs[k * outs_each + h][rows] = part.reshape(step, sub, width)

    outs = pl.pallas_call(
        kernel,
        out_shape=[jax.ShapeDtypeStruct((blocks, sub, width), jnp.float32)] * (count * outs_each),
        grid_spec=pltpu.PrefetchScalarGridSpec(
            num_scalar_prefetch=1,
            grid=(count, blocks // step),
            in_specs=[
                pl.BlockSpec((step, sub, depth), lambda p, g, d: (g, d[p], 0)),
                pl.BlockSpec((depth, across), lambda p, g, d: (0, chunk or 0)),
            ],
            out_specs=[pl.BlockSpec(memory_space=pltpu.VMEM)] * (count * outs_each),
        ),
        cost_estimate=pl.CostEstimate(
            flops=2 * count * blocks * sub * depth * across,
            bytes_accessed=count * blocks * sub * (2 * depth + 4 * across) + 2 * depth * across,
            transcendentals=0,
        ),
        compiler_params=grant(28),
        name="product_pieces",
    )(jnp.stack(dests), panel, sketch)
    return [outs[k * outs_each : (k + 1) * outs_each] for k in range(count)]


def pack_slots(held, inverse, slots):
    children = len(held)
    offsets = inverse.shape[1]
    _, sub, width = held[0].shape

    def kernel(inv_ref, *refs):
        for o in range(offsets):
            out = refs[children + o]

            def fill(j, carry, o=o, out=out):
                total = jnp.zeros((sub, width), jnp.float32)
                for k in range(children):
                    at = inv_ref[(k * offsets + o) * slots + j]
                    block = refs[k][jnp.maximum(at, 0)]
                    total = total + jnp.where(at >= 0, block, 0.0)
                out[j] = total
                return carry

            lax.fori_loop(0, slots, fill, 0)

    moved = 4 * sub * width * slots * offsets * (children + 1)
    return pl.pallas_call(
        kernel,
        out_shape=[jax.ShapeDtypeStruct((slots, sub, width), jnp.float32)] * offsets,
        in_specs=[pl.BlockSpec(memory_space=pltpu.SMEM)] + [pl.BlockSpec(memory_space=pltpu.VMEM)] * children,
        out_specs=[pl.BlockSpec(memory_space=pltpu.VMEM)] * offsets,
        cost_estimate=pl.CostEstimate(flops=moved, bytes_accessed=moved, transcendentals=0),
        compiler_params=grant(12),
        name="pack_slots",
    )(inverse.reshape(-1), *held)


def on_last(a, b):
    return lax.dot_general(a, b, (((1,), (1,)), ((), ())), preferred_element_type=jnp.float32)


def on_first(a, b):
    return lax.dot_general(a, b, (((0,), (0,)), ((), ())), preferred_element_type=jnp.float32)


def plain(a, b):
    return jnp.dot(a, b, preferred_element_type=jnp.float32)


def split(x):
    high = x.astype(jnp.bfloat16)
    return high, (x - high.astype(jnp.float32)).astype(jnp.bfloat16)


def triple(dot, a, b):
    return dot(a[0], b[0]) + (dot(a[0], b[1]) + dot(a[1], b[0]))


def gram_pieces(arrived, here, siblings, members, tile):
    slots, sub, width = arrived[0][0].shape
    rows, n = slots * sub, width * len(arrived)
    count = n // tile
    height = count * (count + 1) // 2 * tile
    piece = height // (siblings * members)
    counts = [len(a) for a in arrived]

    def kernel(here_ref, *refs):
        inputs, (share_ref, *out_refs, packed_ref) = refs[: sum(counts)], refs[sum(counts) :]
        at = 0
        for h, addends in enumerate(counts):
            share_ref[:, h * width : (h + 1) * width] = sum(r[...] for r in inputs[at : at + addends]).reshape(rows, width)
            at += addends
        high, low = split(share_ref[...])
        at = 0
        for i in range(count):
            here, upto = slice(i * tile, (i + 1) * tile), slice(0, (i + 1) * tile)
            strip = triple(on_first, (high[:, here], low[:, here]), (high[:, upto], low[:, upto]))
            for j in range(i + 1):
                packed_ref[at * tile : (at + 1) * tile, :] = strip[:, j * tile : (j + 1) * tile]
                at += 1
        for s in range(siblings):
            for m in range(members):
                spot = ((here_ref[0] ^ s) * members + (here_ref[1] ^ m)) * piece
                out_refs[s][m * piece : (m + 1) * piece, :] = packed_ref[pl.ds(pl.multiple_of(spot, 8), piece), :]

    flat = [x for a in arrived for x in a]
    outs = pl.pallas_call(
        kernel,
        out_shape=[jax.ShapeDtypeStruct((rows, n), jnp.float32)]
        + [jax.ShapeDtypeStruct((members * piece, tile), jnp.float32)] * siblings,
        in_specs=[pl.BlockSpec(memory_space=pltpu.SMEM)] + [pl.BlockSpec(memory_space=pltpu.VMEM)] * len(flat),
        out_specs=[pl.BlockSpec(memory_space=pltpu.VMEM)] * (1 + siblings),
        scratch_shapes=[pltpu.VMEM((height, tile), jnp.float32)],
        cost_estimate=pl.CostEstimate(
            flops=6 * height * tile * rows, bytes_accessed=4 * (len(flat) + 1) * rows * width, transcendentals=0
        ),
        compiler_params=grant(20),
        name="gram_pieces",
    )(here, *flat)
    return outs[0], list(outs[1:])


def basis_pieces(pieces, share, here, siblings, tile):
    rows, n = share.shape
    count = n // tile
    members = len(pieces)
    height = count * (count + 1) // 2 * tile
    piece = height // (siblings * members)
    small, enough = 1e-2, 4e-4

    def kernel(here_ref, *refs):
        piece_refs, share_ref = refs[:members], refs[members]
        out_refs, (packed_ref, g_ref, x_ref, e_ref) = refs[members + 1 : -4], refs[-4:]
        for s in range(siblings):
            for m in range(members):
                spot = ((here_ref[0] ^ s) * members + (here_ref[1] ^ m)) * piece
                packed_ref[pl.ds(pl.multiple_of(spot, 8), piece), :] = piece_refs[m][s * piece : (s + 1) * piece, :]
        at = 0
        for i in range(count):
            here = slice(i * tile, (i + 1) * tile)
            for j in range(i + 1):
                there = slice(j * tile, (j + 1) * tile)
                block = packed_ref[at * tile : (at + 1) * tile, :]
                g_ref[here, there] = block
                if j < i:
                    g_ref[there, here] = block.T
                at += 1
        row_id = lax.broadcasted_iota(jnp.int32, (n, n), 0)
        col_id = lax.broadcasted_iota(jnp.int32, (n, n), 1)

        def eye():
            return jnp.where(row_id == col_id, 1.0, 0.0)

        def half_lower(e):
            rows, columns = row_id[: e.shape[0], : e.shape[1]], col_id[: e.shape[0], : e.shape[1]]
            return jnp.where(rows > columns, e, jnp.where(rows == columns, 0.5 * e, 0.0))

        g = g_ref[...]
        diagonal = jnp.where(row_id == col_id, g, 0.0)
        down = 1.0 / jnp.sqrt(jnp.sum(diagonal, axis=1, keepdims=True))
        across = 1.0 / jnp.sqrt(jnp.sum(diagonal, axis=0, keepdims=True))
        x_ref[...] = jnp.where(row_id == col_id, down, 0.0)
        start = g * down * across - eye()
        e_ref[...] = start

        half = n // 2
        top, low = slice(0, half), slice(half, n)

        def subtract_product(fb, xb):
            x_ref[top, top] = x_ref[top, top] - plain(fb[top, top], xb[top, top])
            x_ref[low, top] = x_ref[low, top] - plain(fb[low, :], xb[:, top])
            x_ref[low, low] = x_ref[low, low] - plain(fb[low, low], xb[low, low])

        def rough(state):
            e = e_ref[...]
            f = half_lower(e)
            fb, eb = f.astype(jnp.bfloat16), e.astype(jnp.bfloat16)
            t = jnp.concatenate([plain(fb[top, top], eb[top, :]), plain(fb[low, :], eb)], axis=0)
            w = (f + t - e).astype(jnp.bfloat16)
            left = on_last(w[:, top], fb[top, top]) - t[:, top]
            right = on_last(w, fb[low, :]) - t[:, low]
            e_ref[:, top] = left
            e_ref[:, low] = right
            subtract_product(fb, x_ref[...].astype(jnp.bfloat16))
            return state[0] + 1, jnp.sum(left * left) + jnp.sum(right * right)

        lax.while_loop(lambda s: (s[0] < 12) & (s[1] > small) & (s[1] < 1e6), rough, (0, jnp.sum(start * start)))

        def fine(state):
            x, g = split(x_ref[...]), split(g_ref[...])

            def cut(pair, rows, columns):
                return pair[0][rows, columns], pair[1][rows, columns]

            every = slice(0, n)
            upper = split(triple(plain, cut(x, top, top), cut(g, top, top)))
            lower = split(triple(plain, cut(x, low, every), g))
            first = cut(x, top, top)
            corner = jnp.where(row_id[top, top] == col_id[top, top], 1.0, 0.0)
            e_top = triple(on_last, upper, first) - corner
            e_side = triple(on_last, cut(lower, every, top), first)
            e_low = triple(on_last, lower, cut(x, low, every)) - corner
            f_top, f_low = half_lower(e_top), half_lower(e_low)
            fb = jnp.concatenate(
                [
                    jnp.concatenate([f_top, jnp.zeros_like(f_top)], axis=1),
                    jnp.concatenate([e_side, f_low], axis=1),
                ],
                axis=0,
            ).astype(jnp.bfloat16)
            subtract_product(fb, x[0])
            size = jnp.sum(e_top * e_top) + 2.0 * jnp.sum(e_side * e_side) + jnp.sum(e_low * e_low)
            return state[0] + 1, size

        _, last = lax.while_loop(
            lambda s: (s[0] < 4) & jnp.logical_not(s[1] < enough), fine, (0, jnp.float32(1.0))
        )

        @pl.when(jnp.logical_not(last < enough))
        def _():
            x_ref[...] = eye()
            e_ref[...] = g_ref[...]
            lane = lax.broadcasted_iota(jnp.int32, (1, n), 1)
            below = lax.broadcasted_iota(jnp.int32, (n, 1), 0)

            def eliminate(j, carry):
                row = e_ref[pl.ds(j, 1), :]
                scale = 1.0 / jnp.sqrt(jnp.sum(jnp.where(lane == j, row, 0.0), axis=1, keepdims=True))
                row = jnp.where(lane > j, row * scale, 0.0)
                solved = x_ref[pl.ds(j, 1), :] * scale
                column = jnp.sum(jnp.where(col_id == j, e_ref[...], 0.0), axis=1, keepdims=True) * scale
                column = jnp.where(below > j, column, 0.0)
                e_ref[...] = e_ref[...] - column * row
                x_ref[...] = x_ref[...] - column * solved
                x_ref[pl.ds(j, 1), :] = solved
                return carry

            lax.fori_loop(0, n, eliminate, 0)

        split_share = split(share_ref[...])
        for i in range(count):
            upto = slice(0, (i + 1) * tile)
            strip = split(x_ref[i * tile : (i + 1) * tile, upto])
            product = triple(on_last, (split_share[0][:, upto], split_share[1][:, upto]), strip)
            for k in range(count):

                @pl.when(here_ref[2] == (i ^ k))
                def _():
                    out_refs[k][...] = product

    return pl.pallas_call(
        kernel,
        out_shape=[jax.ShapeDtypeStruct((rows, tile), jnp.float32)] * count,
        in_specs=[pl.BlockSpec(memory_space=pltpu.SMEM)] + [pl.BlockSpec(memory_space=pltpu.VMEM)] * (1 + members),
        out_specs=[pl.BlockSpec(memory_space=pltpu.VMEM)] * count,
        scratch_shapes=[pltpu.VMEM((height, tile), jnp.float32)] + [pltpu.VMEM((n, n), jnp.float32)] * 3,
        cost_estimate=pl.CostEstimate(flops=12 * n * n * n, bytes_accessed=4 * n * (n + rows), transcendentals=0),
        compiler_params=grant(40),
        name="basis_pieces",
    )(here, *pieces, share)


def lay_out(pieces, here, slots, sub, blk):
    width = pieces[0].shape[1]

    def kernel(here_ref, *refs):
        out_ref, block_ref = refs[-2:]
        for j in range(slots):
            for k in range(len(pieces)):
                spot = pl.ds(pl.multiple_of((here_ref[0] ^ k) * sub, sub), sub)
                block_ref[j, spot, :] = refs[k][j * sub : (j + 1) * sub, :]
        for j in range(slots):
            out_ref[:, j * blk : (j + 1) * blk] = block_ref[j].T

    return pl.pallas_call(
        kernel,
        out_shape=jax.ShapeDtypeStruct((width, slots * blk), jnp.float32),
        in_specs=[pl.BlockSpec(memory_space=pltpu.SMEM)] + [pl.BlockSpec(memory_space=pltpu.VMEM)] * len(pieces),
        out_specs=pl.BlockSpec(memory_space=pltpu.VMEM),
        scratch_shapes=[pltpu.VMEM((slots, blk, width), jnp.float32)],
        compiler_params=grant(12),
        name="lay_out",
    )(here.reshape(1), *pieces)


def shards(child_blocks, sketch, block_map):
    fronts, rows, cols = (lax.axis_size(a) for a in ("front", "row", "col"))
    siblings = min(4, fronts)
    front_here, row_here, col_here = (lax.axis_index(a) for a in ("front", "row", "col"))
    sib_here = front_here % siblings
    total_blocks = block_map.shape[1]
    blocks = total_blocks // rows
    sub = BLK // cols
    sketch_cols = sketch.shape[1]
    parent_blocks = P_SIZE // BLK
    slots = parent_blocks // (siblings * rows)
    spread = parent_blocks - total_blocks
    panel = child_blocks.reshape(blocks, BLK, child_blocks.shape[1])
    both = ("front", "row")

    def place(front, row):
        return front * rows + row

    def may_reach(row, sib, target_row):
        low, high = row * blocks, row * blocks + blocks - 1 + spread
        first = (sib * rows + target_row) * slots
        return low <= first + slots - 1 and first <= high

    maps = [block_map[0]]
    level = 1
    while level < siblings:
        pairs = [(i, i ^ level) for i in range(fronts)]
        maps = maps + [lax.ppermute(m, "front", pairs) for m in maps]
        level *= 2
    own = jnp.stack([lax.dynamic_slice_in_dim(m, row_here * blocks, blocks) for m in maps])
    offset_ids = jnp.arange(rows, dtype=jnp.int32)
    wanted = (sib_here * rows + (row_here ^ offset_ids))[:, None] * slots + jnp.arange(slots, dtype=jnp.int32)[None]
    hit = own[:, None, None, :] == wanted[None, :, :, None]
    inverse = jnp.max(jnp.where(hit, jnp.arange(blocks, dtype=jnp.int32), -1), axis=-1)

    def clipped(dest):
        return jnp.clip(dest, 0, cols - 1)

    wants = []
    for stage in range(1, cols):
        up_dest, down_dest = cols - stage + col_here, stage - cols + col_here
        if stage <= cols // 2:
            wants.append(clipped(jnp.where(up_dest < cols, up_dest, down_dest)))
        else:
            wants += [clipped(up_dest), clipped(down_dest)]
    wants.append(col_here)
    panel = pltpu.with_memory_space_constraint(panel, pltpu.HBM)
    sketch = pltpu.with_memory_space_constraint(sketch, pltpu.HBM)
    products = [[product_pieces(panel, sketch, wants[:1], sub, COLUMN_CHUNKS, h)[0][0] for h in range(COLUMN_CHUNKS)]]
    products += product_pieces(panel, sketch, wants[1:], sub, COLUMN_CHUNKS)

    arrived = []
    for chunk in range(COLUMN_CHUNKS):
        pieces = iter(products)
        came_up = came_down = None
        for stage in range(1, cols):
            up = down = next(pieces)[chunk]
            if stage > cols // 2:
                down = next(pieces)[chunk]
            if came_up is not None:
                up, down = up + came_up, down + came_down
            came_up = lax.ppermute(up, "col", [(i, i + 1) for i in range(stage)])
            came_down = lax.ppermute(down, "col", [(i, i - 1) for i in range(cols - stage, cols)])
        held = [next(pieces)[chunk] + came_up + came_down]
        level = 1
        while level < siblings:
            pairs = [(i, i ^ level) for i in range(fronts)]
            held = held + [lax.ppermute(h, "front", pairs) for h in held]
            level *= 2
        slotted = pack_slots(held, inverse, slots)
        came = [slotted[0]]
        for k in range(1, rows)[::-1]:
            pairs = [
                (place(f, r), place(f, r ^ k))
                for f in range(fronts)
                for r in range(rows)
                if may_reach(r, f % siblings, r ^ k)
            ]
            came.append(lax.ppermute(slotted[k], both, pairs))
        arrived.append(came)

    width = sketch_cols // cols
    here = jnp.stack([sib_here, row_here, col_here])
    share, halves = gram_pieces(arrived, here, siblings, rows, width)

    def swap(x, name, level):
        return lax.ppermute(x, name, [(i, i ^ level) for i in range(lax.axis_size(name))])

    levels = [1 << k for k in range(siblings.bit_length() - 1)]
    kept = dict(enumerate(halves))
    for level in levels:
        kept = {s: kept[s] + swap(kept[s ^ level], "front", level) for s in kept if not s & level}
    parts = kept[0].reshape(rows, kept[0].shape[0] // rows, width)
    piece = parts[0]
    for k in range(1, rows)[::-1]:
        piece = piece + swap(parts[k], "row", k)
    piece = piece + sum(swap(piece, "col", k) for k in range(1, cols)[::-1])
    mine = [piece]
    for level in levels:
        mine = mine + [swap(p, "front", level) for p in mine]
    mine = jnp.concatenate(mine, axis=0)
    pieces = [mine] + [swap(mine, "row", k) for k in range(1, rows)]

    basis = basis_pieces(pieces, share, here, siblings, width)
    pieces = [basis[0]] + [swap(basis[k], "col", k) for k in range(1, cols)]
    return lay_out(pieces, col_here, slots, sub, BLK)


def solution(mesh):
    placed = (P(("front", "row"), "col"), P("col", None), P("front", None))

    return jax.shard_map(shards, mesh=mesh, in_specs=placed, out_specs=P("col", ("front", "row")), check_vma=False)
```

```python
import jax
import jax.numpy as jnp
from jax import lax
from jax.experimental import pallas as pl
from jax.experimental.pallas import tpu as pltpu
from jax.sharding import PartitionSpec as P


P_SIZE = 12288
BLK = 128
COLUMN_CHUNKS = 2


def grant(mebibytes):
    return pltpu.CompilerParams(vmem_limit_bytes=mebibytes << 20)


def product_pieces(panel, sketch, dests, sub, chunks, chunk=None):
    blocks, _, depth = panel.shape
    count = len(dests)
    outs_each = chunks if chunk is None else 1
    width = sketch.shape[1] // chunks
    across = width * outs_each
    step = max(blocks // 2, 1) if chunk is None else max(blocks // 4, 1)

    def kernel(dest_ref, a_ref, b_ref, *outs):
        product = jnp.dot(a_ref[...].reshape(step * sub, depth), b_ref[...], preferred_element_type=jnp.float32)
        rows = pl.ds(pl.program_id(1) * step, step)
        for k in range(count):

            @pl.when(pl.program_id(0) == k)
            def _():
                for h in range(outs_each):
                    part = product[:, h * width : (h + 1) * width]
                    outs[k * outs_each + h][rows] = part.reshape(step, sub, width)

    outs = pl.pallas_call(
        kernel,
        out_shape=[jax.ShapeDtypeStruct((blocks, sub, width), jnp.float32)] * (count * outs_each),
        grid_spec=pltpu.PrefetchScalarGridSpec(
            num_scalar_prefetch=1,
            grid=(count, blocks // step),
            in_specs=[
                pl.BlockSpec((step, sub, depth), lambda p, g, d: (g, d[p], 0)),
                pl.BlockSpec((depth, across), lambda p, g, d: (0, chunk or 0)),
            ],
            out_specs=[pl.BlockSpec(memory_space=pltpu.VMEM)] * (count * outs_each),
        ),
        cost_estimate=pl.CostEstimate(
            flops=2 * count * blocks * sub * depth * across,
            bytes_accessed=count * blocks * sub * (2 * depth + 4 * across) + 2 * depth * across,
            transcendentals=0,
        ),
        compiler_params=grant(28),
        name="product_pieces",
    )(jnp.stack(dests), panel, sketch)
    return [outs[k * outs_each : (k + 1) * outs_each] for k in range(count)]


def pack_slots(held, inverse, slots):
    children = len(held)
    offsets = inverse.shape[1]
    _, sub, width = held[0].shape

    def kernel(inv_ref, *refs):
        for o in range(offsets):
            out = refs[children + o]

            def fill(j, carry, o=o, out=out):
                total = jnp.zeros((sub, width), jnp.float32)
                for k in range(children):
                    at = inv_ref[(k * offsets + o) * slots + j]
                    block = refs[k][jnp.maximum(at, 0)]
                    total = total + jnp.where(at >= 0, block, 0.0)
                out[j] = total
                return carry

            lax.fori_loop(0, slots, fill, 0)

    moved = 4 * sub * width * slots * offsets * (children + 1)
    return pl.pallas_call(
        kernel,
        out_shape=[jax.ShapeDtypeStruct((slots, sub, width), jnp.float32)] * offsets,
        in_specs=[pl.BlockSpec(memory_space=pltpu.SMEM)] + [pl.BlockSpec(memory_space=pltpu.VMEM)] * children,
        out_specs=[pl.BlockSpec(memory_space=pltpu.VMEM)] * offsets,
        cost_estimate=pl.CostEstimate(flops=moved, bytes_accessed=moved, transcendentals=0),
        compiler_params=grant(12),
        name="pack_slots",
    )(inverse.reshape(-1), *held)


def on_last(a, b):
    return lax.dot_general(a, b, (((1,), (1,)), ((), ())), preferred_element_type=jnp.float32)


def on_first(a, b):
    return lax.dot_general(a, b, (((0,), (0,)), ((), ())), preferred_element_type=jnp.float32)


def plain(a, b):
    return jnp.dot(a, b, preferred_element_type=jnp.float32)


def split(x):
    high = x.astype(jnp.bfloat16)
    return high, (x - high.astype(jnp.float32)).astype(jnp.bfloat16)


def triple(dot, a, b):
    return dot(a[0], b[0]) + (dot(a[0], b[1]) + dot(a[1], b[0]))


def gram_pieces(arrived, here, siblings, members, tile):
    slots, sub, width = arrived[0][0].shape
    rows, n = slots * sub, width * len(arrived)
    count = n // tile
    height = count * (count + 1) // 2 * tile
    piece = height // (siblings * members)
    counts = [len(a) for a in arrived]

    def kernel(here_ref, *refs):
        inputs, (share_ref, *out_refs, packed_ref) = refs[: sum(counts)], refs[sum(counts) :]
        at = 0
        for h, addends in enumerate(counts):
            share_ref[:, h * width : (h + 1) * width] = sum(r[...] for r in inputs[at : at + addends]).reshape(rows, width)
            at += addends
        high, low = split(share_ref[...])
        at = 0
        for i in range(count):
            here, upto = slice(i * tile, (i + 1) * tile), slice(0, (i + 1) * tile)
            strip = triple(on_first, (high[:, here], low[:, here]), (high[:, upto], low[:, upto]))
            for j in range(i + 1):
                packed_ref[at * tile : (at + 1) * tile, :] = strip[:, j * tile : (j + 1) * tile]
                at += 1
        for s in range(siblings):
            for m in range(members):
                spot = ((here_ref[0] ^ s) * members + (here_ref[1] ^ m)) * piece
                out_refs[s][m * piece : (m + 1) * piece, :] = packed_ref[pl.ds(pl.multiple_of(spot, 8), piece), :]

    flat = [x for a in arrived for x in a]
    outs = pl.pallas_call(
        kernel,
        out_shape=[jax.ShapeDtypeStruct((rows, n), jnp.float32)]
        + [jax.ShapeDtypeStruct((members * piece, tile), jnp.float32)] * siblings,
        in_specs=[pl.BlockSpec(memory_space=pltpu.SMEM)] + [pl.BlockSpec(memory_space=pltpu.VMEM)] * len(flat),
        out_specs=[pl.BlockSpec(memory_space=pltpu.VMEM)] * (1 + siblings),
        scratch_shapes=[pltpu.VMEM((height, tile), jnp.float32)],
        cost_estimate=pl.CostEstimate(
            flops=6 * height * tile * rows, bytes_accessed=4 * (len(flat) + 1) * rows * width, transcendentals=0
        ),
        compiler_params=grant(20),
        name="gram_pieces",
    )(here, *flat)
    return outs[0], list(outs[1:])


def basis_pieces(pieces, share, here, members, tile):
    rows, n = share.shape
    count = n // tile
    siblings = len(pieces)
    height = count * (count + 1) // 2 * tile
    piece = height // (siblings * members)
    small, enough = 1e-2, 4e-4

    def kernel(here_ref, *refs):
        piece_refs, share_ref = refs[:siblings], refs[siblings]
        out_refs, (packed_ref, g_ref, x_ref, e_ref) = refs[siblings + 1 : -4], refs[-4:]
        for s in range(siblings):
            for m in range(members):
                spot = ((here_ref[0] ^ s) * members + (here_ref[1] ^ m)) * piece
                packed_ref[pl.ds(pl.multiple_of(spot, 8), piece), :] = piece_refs[s][m * piece : (m + 1) * piece, :]
        at = 0
        for i in range(count):
            here = slice(i * tile, (i + 1) * tile)
            for j in range(i + 1):
                there = slice(j * tile, (j + 1) * tile)
                block = packed_ref[at * tile : (at + 1) * tile, :]
                g_ref[here, there] = block
                if j < i:
                    g_ref[there, here] = block.T
                at += 1
        row_id = lax.broadcasted_iota(jnp.int32, (n, n), 0)
        col_id = lax.broadcasted_iota(jnp.int32, (n, n), 1)

        def eye():
            return jnp.where(row_id == col_id, 1.0, 0.0)

        def half_lower(e):
            rows, columns = row_id[: e.shape[0], : e.shape[1]], col_id[: e.shape[0], : e.shape[1]]
            return jnp.where(rows > columns, e, jnp.where(rows == columns, 0.5 * e, 0.0))

        g = g_ref[...]
        diagonal = jnp.where(row_id == col_id, g, 0.0)
        down = 1.0 / jnp.sqrt(jnp.sum(diagonal, axis=1, keepdims=True))
        across = 1.0 / jnp.sqrt(jnp.sum(diagonal, axis=0, keepdims=True))
        x_ref[...] = jnp.where(row_id == col_id, down, 0.0)
        start = g * down * across - eye()
        e_ref[...] = start

        half = n // 2
        top, low = slice(0, half), slice(half, n)

        def subtract_product(fb, xb):
            x_ref[top, top] = x_ref[top, top] - plain(fb[top, top], xb[top, top])
            x_ref[low, top] = x_ref[low, top] - plain(fb[low, :], xb[:, top])
            x_ref[low, low] = x_ref[low, low] - plain(fb[low, low], xb[low, low])

        def rough(state):
            e = e_ref[...]
            f = half_lower(e)
            fb, eb = f.astype(jnp.bfloat16), e.astype(jnp.bfloat16)
            t = jnp.concatenate([plain(fb[top, top], eb[top, :]), plain(fb[low, :], eb)], axis=0)
            w = (f + t - e).astype(jnp.bfloat16)
            left = on_last(w[:, top], fb[top, top]) - t[:, top]
            right = on_last(w, fb[low, :]) - t[:, low]
            e_ref[:, top] = left
            e_ref[:, low] = right
            subtract_product(fb, x_ref[...].astype(jnp.bfloat16))
            return state[0] + 1, jnp.sum(left * left) + jnp.sum(right * right)

        lax.while_loop(lambda s: (s[0] < 12) & (s[1] > small) & (s[1] < 1e6), rough, (0, jnp.sum(start * start)))

        def fine(state):
            x, g = split(x_ref[...]), split(g_ref[...])

            def cut(pair, rows, columns):
                return pair[0][rows, columns], pair[1][rows, columns]

            every = slice(0, n)
            upper = split(triple(plain, cut(x, top, top), cut(g, top, top)))
            lower = split(triple(plain, cut(x, low, every), g))
            first = cut(x, top, top)
            corner = jnp.where(row_id[top, top] == col_id[top, top], 1.0, 0.0)
            e_top = triple(on_last, upper, first) - corner
            e_side = triple(on_last, cut(lower, every, top), first)
            e_low = triple(on_last, lower, cut(x, low, every)) - corner
            f_top, f_low = half_lower(e_top), half_lower(e_low)
            fb = jnp.concatenate(
                [
                    jnp.concatenate([f_top, jnp.zeros_like(f_top)], axis=1),
                    jnp.concatenate([e_side, f_low], axis=1),
                ],
                axis=0,
            ).astype(jnp.bfloat16)
            subtract_product(fb, x[0])
            size = jnp.sum(e_top * e_top) + 2.0 * jnp.sum(e_side * e_side) + jnp.sum(e_low * e_low)
            return state[0] + 1, size

        _, last = lax.while_loop(
            lambda s: (s[0] < 4) & jnp.logical_not(s[1] < enough), fine, (0, jnp.float32(1.0))
        )

        @pl.when(jnp.logical_not(last < enough))
        def _():
            x_ref[...] = eye()
            e_ref[...] = g_ref[...]
            lane = lax.broadcasted_iota(jnp.int32, (1, n), 1)
            below = lax.broadcasted_iota(jnp.int32, (n, 1), 0)

            def eliminate(j, carry):
                row = e_ref[pl.ds(j, 1), :]
                scale = 1.0 / jnp.sqrt(jnp.sum(jnp.where(lane == j, row, 0.0), axis=1, keepdims=True))
                row = jnp.where(lane > j, row * scale, 0.0)
                solved = x_ref[pl.ds(j, 1), :] * scale
                column = jnp.sum(jnp.where(col_id == j, e_ref[...], 0.0), axis=1, keepdims=True) * scale
                column = jnp.where(below > j, column, 0.0)
                e_ref[...] = e_ref[...] - column * row
                x_ref[...] = x_ref[...] - column * solved
                x_ref[pl.ds(j, 1), :] = solved
                return carry

            lax.fori_loop(0, n, eliminate, 0)

        split_share = split(share_ref[...])
        for i in range(count):
            upto = slice(0, (i + 1) * tile)
            strip = split(x_ref[i * tile : (i + 1) * tile, upto])
            product = triple(on_last, (split_share[0][:, upto], split_share[1][:, upto]), strip)
            for k in range(count):

                @pl.when(here_ref[2] == (i ^ k))
                def _():
                    out_refs[k][...] = product

    return pl.pallas_call(
        kernel,
        out_shape=[jax.ShapeDtypeStruct((rows, tile), jnp.float32)] * count,
        in_specs=[pl.BlockSpec(memory_space=pltpu.SMEM)] + [pl.BlockSpec(memory_space=pltpu.VMEM)] * (1 + siblings),
        out_specs=[pl.BlockSpec(memory_space=pltpu.VMEM)] * count,
        scratch_shapes=[pltpu.VMEM((height, tile), jnp.float32)] + [pltpu.VMEM((n, n), jnp.float32)] * 3,
        cost_estimate=pl.CostEstimate(flops=12 * n * n * n, bytes_accessed=4 * n * (n + rows), transcendentals=0),
        compiler_params=grant(40),
        name="basis_pieces",
    )(here, *pieces, share)


def lay_out(pieces, here, slots, sub, blk):
    width = pieces[0].shape[1]

    def kernel(here_ref, *refs):
        out_ref, block_ref = refs[-2:]
        for j in range(slots):
            for k in range(len(pieces)):
                spot = pl.ds(pl.multiple_of((here_ref[0] ^ k) * sub, sub), sub)
                block_ref[j, spot, :] = refs[k][j * sub : (j + 1) * sub, :]
        for j in range(slots):
            out_ref[:, j * blk : (j + 1) * blk] = block_ref[j].T

    return pl.pallas_call(
        kernel,
        out_shape=jax.ShapeDtypeStruct((width, slots * blk), jnp.float32),
        in_specs=[pl.BlockSpec(memory_space=pltpu.SMEM)] + [pl.BlockSpec(memory_space=pltpu.VMEM)] * len(pieces),
        out_specs=pl.BlockSpec(memory_space=pltpu.VMEM),
        scratch_shapes=[pltpu.VMEM((slots, blk, width), jnp.float32)],
        compiler_params=grant(12),
        name="lay_out",
    )(here.reshape(1), *pieces)


def shards(child_blocks, sketch, block_map):
    fronts, rows, cols = (lax.axis_size(a) for a in ("front", "row", "col"))
    siblings = min(4, fronts)
    front_here, row_here, col_here = (lax.axis_index(a) for a in ("front", "row", "col"))
    sib_here = front_here % siblings
    total_blocks = block_map.shape[1]
    blocks = total_blocks // rows
    sub = BLK // cols
    sketch_cols = sketch.shape[1]
    parent_blocks = P_SIZE // BLK
    slots = parent_blocks // (siblings * rows)
    spread = parent_blocks - total_blocks
    panel = child_blocks.reshape(blocks, BLK, child_blocks.shape[1])
    both = ("front", "row")

    def place(front, row):
        return front * rows + row

    def may_reach(row, sib, target_row):
        low, high = row * blocks, row * blocks + blocks - 1 + spread
        first = (sib * rows + target_row) * slots
        return low <= first + slots - 1 and first <= high

    maps = [block_map[0]]
    level = 1
    while level < siblings:
        pairs = [(i, i ^ level) for i in range(fronts)]
        maps = maps + [lax.ppermute(m, "front", pairs) for m in maps]
        level *= 2
    own = jnp.stack([lax.dynamic_slice_in_dim(m, row_here * blocks, blocks) for m in maps])
    offset_ids = jnp.arange(rows, dtype=jnp.int32)
    wanted = (sib_here * rows + (row_here ^ offset_ids))[:, None] * slots + jnp.arange(slots, dtype=jnp.int32)[None]
    hit = own[:, None, None, :] == wanted[None, :, :, None]
    inverse = jnp.max(jnp.where(hit, jnp.arange(blocks, dtype=jnp.int32), -1), axis=-1)

    def clipped(dest):
        return jnp.clip(dest, 0, cols - 1)

    wants = []
    for stage in range(1, cols):
        up_dest, down_dest = cols - stage + col_here, stage - cols + col_here
        if stage <= cols // 2:
            wants.append(clipped(jnp.where(up_dest < cols, up_dest, down_dest)))
        else:
            wants += [clipped(up_dest), clipped(down_dest)]
    wants.append(col_here)
    panel = pltpu.with_memory_space_constraint(panel, pltpu.HBM)
    sketch = pltpu.with_memory_space_constraint(sketch, pltpu.HBM)
    products = [[product_pieces(panel, sketch, wants[:1], sub, COLUMN_CHUNKS, h)[0][0] for h in range(COLUMN_CHUNKS)]]
    products += product_pieces(panel, sketch, wants[1:], sub, COLUMN_CHUNKS)

    arrived = []
    for chunk in range(COLUMN_CHUNKS):
        pieces = iter(products)
        came_up = came_down = None
        for stage in range(1, cols):
            up = down = next(pieces)[chunk]
            if stage > cols // 2:
                down = next(pieces)[chunk]
            if came_up is not None:
                up, down = up + came_up, down + came_down
            came_up = lax.ppermute(up, "col", [(i, i + 1) for i in range(stage)])
            came_down = lax.ppermute(down, "col", [(i, i - 1) for i in range(cols - stage, cols)])
        held = [next(pieces)[chunk] + came_up + came_down]
        level = 1
        while level < siblings:
            pairs = [(i, i ^ level) for i in range(fronts)]
            held = held + [lax.ppermute(h, "front", pairs) for h in held]
            level *= 2
        slotted = pack_slots(held, inverse, slots)
        came = [slotted[0]]
        for k in range(1, rows)[::-1]:
            pairs = [
                (place(f, r), place(f, r ^ k))
                for f in range(fronts)
                for r in range(rows)
                if may_reach(r, f % siblings, r ^ k)
            ]
            came.append(lax.ppermute(slotted[k], both, pairs))
        arrived.append(came)

    width = sketch_cols // cols
    here = jnp.stack([sib_here, row_here, col_here])
    share, halves = gram_pieces(arrived, here, siblings, rows, width)

    def swap(x, name, level):
        return lax.ppermute(x, name, [(i, i ^ level) for i in range(lax.axis_size(name))])

    levels = [1 << k for k in range(siblings.bit_length() - 1)]
    kept = dict(enumerate(halves))
    for level in levels:
        kept = {s: kept[s] + swap(kept[s ^ level], "front", level) for s in kept if not s & level}
    parts = kept[0].reshape(rows, kept[0].shape[0] // rows, width)
    piece = parts[0]
    for k in range(1, rows)[::-1]:
        piece = piece + swap(parts[k], "row", k)
    piece = piece + sum(swap(piece, "col", k) for k in range(1, cols)[::-1])
    back = {0: piece}
    for k in range(1, rows)[::-1]:
        back[k] = swap(piece, "row", k)
    pieces = [jnp.concatenate([back[k] for k in range(rows)], axis=0)]
    for level in levels:
        pieces = pieces + [swap(p, "front", level) for p in pieces]

    basis = basis_pieces(pieces, share, here, rows, width)
    came = {k: swap(basis[k], "col", k) for k in range(1, cols)[::-1]}
    pieces = [basis[0]] + [came[k] for k in range(1, cols)]
    return lay_out(pieces, col_here, slots, sub, BLK)


def solution(mesh):
    placed = (P(("front", "row"), "col"), P("col", None), P("front", None))

    return jax.shard_map(shards, mesh=mesh, in_specs=placed, out_specs=P("col", ("front", "row")), check_vma=False)
```

```python
import jax
import jax.numpy as jnp
from jax import lax
from jax.experimental import pallas as pl
from jax.experimental.pallas import tpu as pltpu
from jax.sharding import PartitionSpec as P


P_SIZE = 12288
BLK = 128
COLUMN_CHUNKS = 2


def grant(mebibytes):
    return pltpu.CompilerParams(vmem_limit_bytes=mebibytes << 20)


def product_pieces(panel, sketch, dests, sub, chunks, chunk=None):
    blocks, _, depth = panel.shape
    count = len(dests)
    outs_each = chunks if chunk is None else 1
    width = sketch.shape[1] // chunks
    across = width * outs_each
    step = max(blocks // 2, 1)
    fetches = 4 if step % 4 == 0 else 1
    fetched = step // fetches

    def kernel(dest_ref, *refs):
        a_refs, b_ref, outs = refs[:fetches], refs[fetches], refs[fetches + 1 :]
        a = jnp.concatenate([r[...].reshape(fetched * sub, depth) for r in a_refs], axis=0)
        product = jnp.dot(a, b_ref[...], preferred_element_type=jnp.float32)
        rows = pl.ds(pl.program_id(1) * step, step)
        for k in range(count):

            @pl.when(pl.program_id(0) == k)
            def _():
                for h in range(outs_each):
                    part = product[:, h * width : (h + 1) * width]
                    outs[k * outs_each + h][rows] = part.reshape(step, sub, width)

    outs = pl.pallas_call(
        kernel,
        out_shape=[jax.ShapeDtypeStruct((blocks, sub, width), jnp.float32)] * (count * outs_each),
        grid_spec=pltpu.PrefetchScalarGridSpec(
            num_scalar_prefetch=1,
            grid=(count, blocks // step),
            in_specs=[
                pl.BlockSpec((fetched, sub, depth), lambda p, g, d, i=i: (g * fetches + i, d[p], 0))
                for i in range(fetches)
            ]
            + [
                pl.BlockSpec((depth, across), lambda p, g, d: (0, chunk or 0)),
            ],
            out_specs=[pl.BlockSpec(memory_space=pltpu.VMEM)] * (count * outs_each),
        ),
        cost_estimate=pl.CostEstimate(
            flops=2 * count * blocks * sub * depth * across,
            bytes_accessed=count * blocks * sub * (2 * depth + 4 * across) + 2 * depth * across,
            transcendentals=0,
        ),
        compiler_params=grant(28),
        name="product_pieces",
    )(jnp.stack(dests), *[panel] * fetches, sketch)
    return [outs[k * outs_each : (k + 1) * outs_each] for k in range(count)]


def pack_slots(held, inverse, slots):
    children = len(held)
    offsets = inverse.shape[1]
    _, sub, width = held[0].shape

    def kernel(inv_ref, *refs):
        for o in range(offsets):
            out = refs[children + o]

            def fill(j, carry, o=o, out=out):
                total = jnp.zeros((sub, width), jnp.float32)
                for k in range(children):
                    at = inv_ref[(k * offsets + o) * slots + j]
                    block = refs[k][jnp.maximum(at, 0)]
                    total = total + jnp.where(at >= 0, block, 0.0)
                out[j] = total
                return carry

            lax.fori_loop(0, slots, fill, 0)

    moved = 4 * sub * width * slots * offsets * (children + 1)
    return pl.pallas_call(
        kernel,
        out_shape=[jax.ShapeDtypeStruct((slots, sub, width), jnp.float32)] * offsets,
        in_specs=[pl.BlockSpec(memory_space=pltpu.SMEM)] + [pl.BlockSpec(memory_space=pltpu.VMEM)] * children,
        out_specs=[pl.BlockSpec(memory_space=pltpu.VMEM)] * offsets,
        cost_estimate=pl.CostEstimate(flops=moved, bytes_accessed=moved, transcendentals=0),
        compiler_params=grant(12),
        name="pack_slots",
    )(inverse.reshape(-1), *held)


def on_last(a, b):
    return lax.dot_general(a, b, (((1,), (1,)), ((), ())), preferred_element_type=jnp.float32)


def on_first(a, b):
    return lax.dot_general(a, b, (((0,), (0,)), ((), ())), preferred_element_type=jnp.float32)


def plain(a, b):
    return jnp.dot(a, b, preferred_element_type=jnp.float32)


def split(x):
    high = x.astype(jnp.bfloat16)
    return high, (x - high.astype(jnp.float32)).astype(jnp.bfloat16)


def triple(dot, a, b):
    return dot(a[0], b[0]) + (dot(a[0], b[1]) + dot(a[1], b[0]))


def gram_pieces(arrived, here, siblings, members, tile):
    slots, sub, width = arrived[0][0].shape
    rows, n = slots * sub, width * len(arrived)
    count = n // tile
    height = count * (count + 1) // 2 * tile
    piece = height // (siblings * members)
    counts = [len(a) for a in arrived]

    def kernel(here_ref, *refs):
        inputs, (share_ref, *out_refs, packed_ref) = refs[: sum(counts)], refs[sum(counts) :]
        at = 0
        for h, addends in enumerate(counts):
            share_ref[:, h * width : (h + 1) * width] = sum(r[...] for r in inputs[at : at + addends]).reshape(rows, width)
            at += addends
        high, low = split(share_ref[...])
        at = 0
        for i in range(count):
            here, upto = slice(i * tile, (i + 1) * tile), slice(0, (i + 1) * tile)
            strip = triple(on_first, (high[:, here], low[:, here]), (high[:, upto], low[:, upto]))
            for j in range(i + 1):
                packed_ref[at * tile : (at + 1) * tile, :] = strip[:, j * tile : (j + 1) * tile]
                at += 1
        for s in range(siblings):
            for m in range(members):
                spot = ((here_ref[0] ^ s) * members + (here_ref[1] ^ m)) * piece
                out_refs[s][m * piece : (m + 1) * piece, :] = packed_ref[pl.ds(pl.multiple_of(spot, 8), piece), :]

    flat = [x for a in arrived for x in a]
    outs = pl.pallas_call(
        kernel,
        out_shape=[jax.ShapeDtypeStruct((rows, n), jnp.float32)]
        + [jax.ShapeDtypeStruct((members * piece, tile), jnp.float32)] * siblings,
        in_specs=[pl.BlockSpec(memory_space=pltpu.SMEM)] + [pl.BlockSpec(memory_space=pltpu.VMEM)] * len(flat),
        out_specs=[pl.BlockSpec(memory_space=pltpu.VMEM)] * (1 + siblings),
        scratch_shapes=[pltpu.VMEM((height, tile), jnp.float32)],
        cost_estimate=pl.CostEstimate(
            flops=6 * height * tile * rows, bytes_accessed=4 * (len(flat) + 1) * rows * width, transcendentals=0
        ),
        compiler_params=grant(20),
        name="gram_pieces",
    )(here, *flat)
    return outs[0], list(outs[1:])


def basis_pieces(pieces, share, here, members, tile):
    rows, n = share.shape
    count = n // tile
    siblings = len(pieces)
    height = count * (count + 1) // 2 * tile
    piece = height // (siblings * members)
    small, enough = 1e-2, 4e-4

    def kernel(here_ref, *refs):
        piece_refs, share_ref = refs[:siblings], refs[siblings]
        out_refs, (packed_ref, g_ref, x_ref, e_ref) = refs[siblings + 1 : -4], refs[-4:]
        for s in range(siblings):
            for m in range(members):
                spot = ((here_ref[0] ^ s) * members + (here_ref[1] ^ m)) * piece
                packed_ref[pl.ds(pl.multiple_of(spot, 8), piece), :] = piece_refs[s][m * piece : (m + 1) * piece, :]
        at = 0
        for i in range(count):
            here = slice(i * tile, (i + 1) * tile)
            for j in range(i + 1):
                there = slice(j * tile, (j + 1) * tile)
                block = packed_ref[at * tile : (at + 1) * tile, :]
                g_ref[here, there] = block
                if j < i:
                    g_ref[there, here] = block.T
                at += 1
        row_id = lax.broadcasted_iota(jnp.int32, (n, n), 0)
        col_id = lax.broadcasted_iota(jnp.int32, (n, n), 1)

        def eye():
            return jnp.where(row_id == col_id, 1.0, 0.0)

        def half_lower(e):
            rows, columns = row_id[: e.shape[0], : e.shape[1]], col_id[: e.shape[0], : e.shape[1]]
            return jnp.where(rows > columns, e, jnp.where(rows == columns, 0.5 * e, 0.0))

        g = g_ref[...]
        diagonal = jnp.where(row_id == col_id, g, 0.0)
        down = 1.0 / jnp.sqrt(jnp.sum(diagonal, axis=1, keepdims=True))
        across = 1.0 / jnp.sqrt(jnp.sum(diagonal, axis=0, keepdims=True))
        x_ref[...] = jnp.where(row_id == col_id, down, 0.0)
        start = g * down * across - eye()
        e_ref[...] = start

        half = n // 2
        top, low = slice(0, half), slice(half, n)

        def subtract_product(fb, xb):
            x_ref[top, top] = x_ref[top, top] - plain(fb[top, top], xb[top, top])
            x_ref[low, top] = x_ref[low, top] - plain(fb[low, :], xb[:, top])
            x_ref[low, low] = x_ref[low, low] - plain(fb[low, low], xb[low, low])

        def rough(state):
            e = e_ref[...]
            f = half_lower(e)
            fb, eb = f.astype(jnp.bfloat16), e.astype(jnp.bfloat16)
            t = jnp.concatenate([plain(fb[top, top], eb[top, :]), plain(fb[low, :], eb)], axis=0)
            w = (f + t - e).astype(jnp.bfloat16)
            left = on_last(w[:, top], fb[top, top]) - t[:, top]
            right = on_last(w, fb[low, :]) - t[:, low]
            e_ref[:, top] = left
            e_ref[:, low] = right
            subtract_product(fb, x_ref[...].astype(jnp.bfloat16))
            return state[0] + 1, jnp.sum(left * left) + jnp.sum(right * right)

        lax.while_loop(lambda s: (s[0] < 12) & (s[1] > small) & (s[1] < 1e6), rough, (0, jnp.sum(start * start)))

        def fine(state):
            x, g = split(x_ref[...]), split(g_ref[...])

            def cut(pair, rows, columns):
                return pair[0][rows, columns], pair[1][rows, columns]

            every = slice(0, n)
            upper = split(triple(plain, cut(x, top, top), cut(g, top, top)))
            lower = split(triple(plain, cut(x, low, every), g))
            first = cut(x, top, top)
            corner = jnp.where(row_id[top, top] == col_id[top, top], 1.0, 0.0)
            e_top = triple(on_last, upper, first) - corner
            e_side = triple(on_last, cut(lower, every, top), first)
            e_low = triple(on_last, lower, cut(x, low, every)) - corner
            f_top, f_low = half_lower(e_top), half_lower(e_low)
            fb = jnp.concatenate(
                [
                    jnp.concatenate([f_top, jnp.zeros_like(f_top)], axis=1),
                    jnp.concatenate([e_side, f_low], axis=1),
                ],
                axis=0,
            ).astype(jnp.bfloat16)
            subtract_product(fb, x[0])
            size = jnp.sum(e_top * e_top) + 2.0 * jnp.sum(e_side * e_side) + jnp.sum(e_low * e_low)
            return state[0] + 1, size

        _, last = lax.while_loop(
            lambda s: (s[0] < 4) & jnp.logical_not(s[1] < enough), fine, (0, jnp.float32(1.0))
        )

        @pl.when(jnp.logical_not(last < enough))
        def _():
            x_ref[...] = eye()
            e_ref[...] = g_ref[...]
            lane = lax.broadcasted_iota(jnp.int32, (1, n), 1)
            below = lax.broadcasted_iota(jnp.int32, (n, 1), 0)

            def eliminate(j, carry):
                row = e_ref[pl.ds(j, 1), :]
                scale = 1.0 / jnp.sqrt(jnp.sum(jnp.where(lane == j, row, 0.0), axis=1, keepdims=True))
                row = jnp.where(lane > j, row * scale, 0.0)
                solved = x_ref[pl.ds(j, 1), :] * scale
                column = jnp.sum(jnp.where(col_id == j, e_ref[...], 0.0), axis=1, keepdims=True) * scale
                column = jnp.where(below > j, column, 0.0)
                e_ref[...] = e_ref[...] - column * row
                x_ref[...] = x_ref[...] - column * solved
                x_ref[pl.ds(j, 1), :] = solved
                return carry

            lax.fori_loop(0, n, eliminate, 0)

        split_share = split(share_ref[...])
        for i in range(count):
            upto = slice(0, (i + 1) * tile)
            strip = split(x_ref[i * tile : (i + 1) * tile, upto])
            product = triple(on_last, (split_share[0][:, upto], split_share[1][:, upto]), strip)
            for k in range(count):

                @pl.when(here_ref[2] == (i ^ k))
                def _():
                    out_refs[k][...] = product

    return pl.pallas_call(
        kernel,
        out_shape=[jax.ShapeDtypeStruct((rows, tile), jnp.float32)] * count,
        in_specs=[pl.BlockSpec(memory_space=pltpu.SMEM)] + [pl.BlockSpec(memory_space=pltpu.VMEM)] * (1 + siblings),
        out_specs=[pl.BlockSpec(memory_space=pltpu.VMEM)] * count,
        scratch_shapes=[pltpu.VMEM((height, tile), jnp.float32)] + [pltpu.VMEM((n, n), jnp.float32)] * 3,
        cost_estimate=pl.CostEstimate(flops=12 * n * n * n, bytes_accessed=4 * n * (n + rows), transcendentals=0),
        compiler_params=grant(40),
        name="basis_pieces",
    )(here, *pieces, share)


def lay_out(pieces, here, slots, sub, blk):
    width = pieces[0].shape[1]

    def kernel(here_ref, *refs):
        out_ref, block_ref = refs[-2:]
        for j in range(slots):
            for k in range(len(pieces)):
                spot = pl.ds(pl.multiple_of((here_ref[0] ^ k) * sub, sub), sub)
                block_ref[j, spot, :] = refs[k][j * sub : (j + 1) * sub, :]
        for j in range(slots):
            out_ref[:, j * blk : (j + 1) * blk] = block_ref[j].T

    return pl.pallas_call(
        kernel,
        out_shape=jax.ShapeDtypeStruct((width, slots * blk), jnp.float32),
        in_specs=[pl.BlockSpec(memory_space=pltpu.SMEM)] + [pl.BlockSpec(memory_space=pltpu.VMEM)] * len(pieces),
        out_specs=pl.BlockSpec(memory_space=pltpu.VMEM),
        scratch_shapes=[pltpu.VMEM((slots, blk, width), jnp.float32)],
        compiler_params=grant(12),
        name="lay_out",
    )(here.reshape(1), *pieces)


def shards(child_blocks, sketch, block_map):
    fronts, rows, cols = (lax.axis_size(a) for a in ("front", "row", "col"))
    siblings = min(4, fronts)
    front_here, row_here, col_here = (lax.axis_index(a) for a in ("front", "row", "col"))
    sib_here = front_here % siblings
    total_blocks = block_map.shape[1]
    blocks = total_blocks // rows
    sub = BLK // cols
    sketch_cols = sketch.shape[1]
    parent_blocks = P_SIZE // BLK
    slots = parent_blocks // (siblings * rows)
    spread = parent_blocks - total_blocks
    panel = child_blocks.reshape(blocks, BLK, child_blocks.shape[1])
    both = ("front", "row")

    def place(front, row):
        return front * rows + row

    def may_reach(row, sib, target_row):
        low, high = row * blocks, row * blocks + blocks - 1 + spread
        first = (sib * rows + target_row) * slots
        return low <= first + slots - 1 and first <= high

    maps = [block_map[0]]
    level = 1
    while level < siblings:
        pairs = [(i, i ^ level) for i in range(fronts)]
        maps = maps + [lax.ppermute(m, "front", pairs) for m in maps]
        level *= 2
    own = jnp.stack([lax.dynamic_slice_in_dim(m, row_here * blocks, blocks) for m in maps])
    offset_ids = jnp.arange(rows, dtype=jnp.int32)
    wanted = (sib_here * rows + (row_here ^ offset_ids))[:, None] * slots + jnp.arange(slots, dtype=jnp.int32)[None]
    hit = own[:, None, None, :] == wanted[None, :, :, None]
    inverse = jnp.max(jnp.where(hit, jnp.arange(blocks, dtype=jnp.int32), -1), axis=-1)

    def clipped(dest):
        return jnp.clip(dest, 0, cols - 1)

    wants = []
    for stage in range(1, cols):
        up_dest, down_dest = cols - stage + col_here, stage - cols + col_here
        if stage <= cols // 2:
            wants.append(clipped(jnp.where(up_dest < cols, up_dest, down_dest)))
        else:
            wants += [clipped(up_dest), clipped(down_dest)]
    wants.append(col_here)
    panel = pltpu.with_memory_space_constraint(panel, pltpu.HBM)
    sketch = pltpu.with_memory_space_constraint(sketch, pltpu.HBM)
    ends = (col_here == 0) | (col_here == cols - 1)

    def first_piece(chunk):
        return product_pieces(panel, sketch, wants[:1], sub, COLUMN_CHUNKS, chunk)[0][0]

    def no_piece():
        return jnp.zeros((blocks, sub, sketch_cols // COLUMN_CHUNKS), jnp.float32)

    products = [[lax.cond(ends, lambda h=h: first_piece(h), no_piece) for h in range(COLUMN_CHUNKS)]]
    products += product_pieces(panel, sketch, wants[1:], sub, COLUMN_CHUNKS)

    arrived = []
    for chunk in range(COLUMN_CHUNKS):
        pieces = iter(products)
        came_up = came_down = None
        for stage in range(1, cols):
            up = down = next(pieces)[chunk]
            if stage > cols // 2:
                down = next(pieces)[chunk]
            if came_up is not None:
                up, down = up + came_up, down + came_down
            came_up = lax.ppermute(up, "col", [(i, i + 1) for i in range(stage)])
            came_down = lax.ppermute(down, "col", [(i, i - 1) for i in range(cols - stage, cols)])
        held = [next(pieces)[chunk] + came_up + came_down]
        level = 1
        while level < siblings:
            pairs = [(i, i ^ level) for i in range(fronts)]
            held = held + [lax.ppermute(h, "front", pairs) for h in held]
            level *= 2
        slotted = pack_slots(held, inverse, slots)
        came = [slotted[0]]
        for k in range(1, rows)[::-1]:
            pairs = [
                (place(f, r), place(f, r ^ k))
                for f in range(fronts)
                for r in range(rows)
                if may_reach(r, f % siblings, r ^ k)
            ]
            came.append(lax.ppermute(slotted[k], both, pairs))
        arrived.append(came)

    width = sketch_cols // cols
    here = jnp.stack([sib_here, row_here, col_here])
    share, halves = gram_pieces(arrived, here, siblings, rows, width)

    def swap(x, name, level):
        return lax.ppermute(x, name, [(i, i ^ level) for i in range(lax.axis_size(name))])

    levels = [1 << k for k in range(siblings.bit_length() - 1)]
    kept = dict(enumerate(halves))
    for level in levels:
        kept = {s: kept[s] + swap(kept[s ^ level], "front", level) for s in kept if not s & level}
    parts = kept[0].reshape(rows, kept[0].shape[0] // rows, width)
    piece = parts[0]
    for k in range(1, rows)[::-1]:
        piece = piece + swap(parts[k], "row", k)
    piece = piece + sum(swap(piece, "col", k) for k in range(1, cols)[::-1])
    back = {0: piece}
    for k in range(1, rows)[::-1]:
        back[k] = swap(piece, "row", k)
    pieces = [jnp.concatenate([back[k] for k in range(rows)], axis=0)]
    for level in levels:
        pieces = pieces + [swap(p, "front", level) for p in pieces]

    basis = basis_pieces(pieces, share, here, rows, width)
    came = {k: swap(basis[k], "col", k) for k in range(1, cols)[::-1]}
    pieces = [basis[0]] + [came[k] for k in range(1, cols)]
    return lay_out(pieces, col_here, slots, sub, BLK)


def solution(mesh):
    placed = (P(("front", "row"), "col"), P("col", None), P("front", None))

    return jax.shard_map(shards, mesh=mesh, in_specs=placed, out_specs=P("col", ("front", "row")), check_vma=False)
```

```python
import jax
import jax.numpy as jnp
from jax import lax
from jax.experimental import pallas as pl
from jax.experimental.pallas import tpu as pltpu
from jax.sharding import PartitionSpec as P


P_SIZE = 12288
BLK = 128
COLUMN_CHUNKS = 2


def grant(mebibytes):
    return pltpu.CompilerParams(vmem_limit_bytes=mebibytes << 20)


def product_pieces(panel, sketch, dests, sub, chunks, chunk=None):
    blocks, _, depth = panel.shape
    count = len(dests)
    outs_each = chunks if chunk is None else 1
    width = sketch.shape[1] // chunks
    across = width * outs_each
    step = max(blocks // 2, 1)
    fetches = 4 if step % 4 == 0 else 1
    fetched = step // fetches

    def kernel(dest_ref, *refs):
        a_refs, b_ref, outs = refs[:fetches], refs[fetches], refs[fetches + 1 :]
        a = jnp.concatenate([r[...].reshape(fetched * sub, depth) for r in a_refs], axis=0)
        product = jnp.dot(a, b_ref[...], preferred_element_type=jnp.float32)
        rows = pl.ds(pl.program_id(1) * step, step)
        for k in range(count):

            @pl.when(pl.program_id(0) == k)
            def _():
                for h in range(outs_each):
                    part = product[:, h * width : (h + 1) * width]
                    outs[k * outs_each + h][rows] = part.reshape(step, sub, width)

    outs = pl.pallas_call(
        kernel,
        out_shape=[jax.ShapeDtypeStruct((blocks, sub, width), jnp.float32)] * (count * outs_each),
        grid_spec=pltpu.PrefetchScalarGridSpec(
            num_scalar_prefetch=1,
            grid=(count, blocks // step),
            in_specs=[
                pl.BlockSpec((fetched, sub, depth), lambda p, g, d, i=i: (g * fetches + i, d[p], 0))
                for i in range(fetches)
            ]
            + [
                pl.BlockSpec((depth, across), lambda p, g, d: (0, chunk or 0)),
            ],
            out_specs=[pl.BlockSpec(memory_space=pltpu.VMEM)] * (count * outs_each),
        ),
        cost_estimate=pl.CostEstimate(
            flops=2 * count * blocks * sub * depth * across,
            bytes_accessed=count * blocks * sub * (2 * depth + 4 * across) + 2 * depth * across,
            transcendentals=0,
        ),
        compiler_params=grant(18),
        name="product_pieces",
    )(jnp.stack(dests), *[panel] * fetches, sketch)
    return [outs[k * outs_each : (k + 1) * outs_each] for k in range(count)]


def pack_slots(held, inverse, slots):
    children = len(held)
    offsets = inverse.shape[1]
    _, sub, width = held[0].shape

    def kernel(inv_ref, *refs):
        for o in range(offsets):
            out = refs[children + o]

            def fill(j, carry, o=o, out=out):
                total = jnp.zeros((sub, width), jnp.float32)
                for k in range(children):
                    at = inv_ref[(k * offsets + o) * slots + j]
                    block = refs[k][jnp.maximum(at, 0)]
                    total = total + jnp.where(at >= 0, block, 0.0)
                out[j] = total
                return carry

            lax.fori_loop(0, slots, fill, 0)

    moved = 4 * sub * width * slots * offsets * (children + 1)
    return pl.pallas_call(
        kernel,
        out_shape=[jax.ShapeDtypeStruct((slots, sub, width), jnp.float32)] * offsets,
        in_specs=[pl.BlockSpec(memory_space=pltpu.SMEM)] + [pl.BlockSpec(memory_space=pltpu.VMEM)] * children,
        out_specs=[pl.BlockSpec(memory_space=pltpu.VMEM)] * offsets,
        cost_estimate=pl.CostEstimate(flops=moved, bytes_accessed=moved, transcendentals=0),
        compiler_params=grant(12),
        name="pack_slots",
    )(inverse.reshape(-1), *held)


def on_last(a, b):
    return lax.dot_general(a, b, (((1,), (1,)), ((), ())), preferred_element_type=jnp.float32)


def on_first(a, b):
    return lax.dot_general(a, b, (((0,), (0,)), ((), ())), preferred_element_type=jnp.float32)


def plain(a, b):
    return jnp.dot(a, b, preferred_element_type=jnp.float32)


def split(x):
    high = x.astype(jnp.bfloat16)
    return high, (x - high.astype(jnp.float32)).astype(jnp.bfloat16)


def triple(dot, a, b):
    return dot(a[0], b[0]) + (dot(a[0], b[1]) + dot(a[1], b[0]))


def gram_pieces(arrived, here, siblings, members, tile):
    slots, sub, width = arrived[0][0].shape
    rows, n = slots * sub, width * len(arrived)
    count = n // tile
    height = count * (count + 1) // 2 * tile
    piece = height // (siblings * members)
    counts = [len(a) for a in arrived]

    def kernel(here_ref, *refs):
        inputs, (share_ref, *out_refs, packed_ref) = refs[: sum(counts)], refs[sum(counts) :]
        at = 0
        for h, addends in enumerate(counts):
            share_ref[:, h * width : (h + 1) * width] = sum(r[...] for r in inputs[at : at + addends]).reshape(rows, width)
            at += addends
        high, low = split(share_ref[...])
        at = 0
        for i in range(count):
            here, upto = slice(i * tile, (i + 1) * tile), slice(0, (i + 1) * tile)
            strip = triple(on_first, (high[:, here], low[:, here]), (high[:, upto], low[:, upto]))
            for j in range(i + 1):
                packed_ref[at * tile : (at + 1) * tile, :] = strip[:, j * tile : (j + 1) * tile]
                at += 1
        for s in range(siblings):
            for m in range(members):
                spot = ((here_ref[0] ^ s) * members + (here_ref[1] ^ m)) * piece
                out_refs[s][m * piece : (m + 1) * piece, :] = packed_ref[pl.ds(pl.multiple_of(spot, 8), piece), :]

    flat = [x for a in arrived for x in a]
    outs = pl.pallas_call(
        kernel,
        out_shape=[jax.ShapeDtypeStruct((rows, n), jnp.float32)]
        + [jax.ShapeDtypeStruct((members * piece, tile), jnp.float32)] * siblings,
        in_specs=[pl.BlockSpec(memory_space=pltpu.SMEM)] + [pl.BlockSpec(memory_space=pltpu.VMEM)] * len(flat),
        out_specs=[pl.BlockSpec(memory_space=pltpu.VMEM)] * (1 + siblings),
        scratch_shapes=[pltpu.VMEM((height, tile), jnp.float32)],
        cost_estimate=pl.CostEstimate(
            flops=6 * height * tile * rows, bytes_accessed=4 * (len(flat) + 1) * rows * width, transcendentals=0
        ),
        compiler_params=grant(20),
        name="gram_pieces",
    )(here, *flat)
    return outs[0], list(outs[1:])


def basis_pieces(pieces, share, here, members, tile):
    rows, n = share.shape
    count = n // tile
    siblings = len(pieces)
    height = count * (count + 1) // 2 * tile
    piece = height // (siblings * members)
    small, enough = 1e-2, 4e-4

    def kernel(here_ref, *refs):
        piece_refs, share_ref = refs[:siblings], refs[siblings]
        out_refs, strip_ref = refs[siblings + 1 : -5], refs[-5]
        packed_ref, g_ref, x_ref, e_ref = refs[-4:]
        for s in range(siblings):
            for m in range(members):
                spot = ((here_ref[0] ^ s) * members + (here_ref[1] ^ m)) * piece
                packed_ref[pl.ds(pl.multiple_of(spot, 8), piece), :] = piece_refs[s][m * piece : (m + 1) * piece, :]
        at = 0
        for i in range(count):
            here = slice(i * tile, (i + 1) * tile)
            for j in range(i + 1):
                there = slice(j * tile, (j + 1) * tile)
                block = packed_ref[at * tile : (at + 1) * tile, :]
                g_ref[here, there] = block
                if j < i:
                    g_ref[there, here] = block.T
                at += 1
        row_id = lax.broadcasted_iota(jnp.int32, (n, n), 0)
        col_id = lax.broadcasted_iota(jnp.int32, (n, n), 1)

        def eye():
            return jnp.where(row_id == col_id, 1.0, 0.0)

        def half_lower(e):
            rows, columns = row_id[: e.shape[0], : e.shape[1]], col_id[: e.shape[0], : e.shape[1]]
            return jnp.where(rows > columns, e, jnp.where(rows == columns, 0.5 * e, 0.0))

        g = g_ref[...]
        diagonal = jnp.where(row_id == col_id, g, 0.0)
        down = 1.0 / jnp.sqrt(jnp.sum(diagonal, axis=1, keepdims=True))
        across = 1.0 / jnp.sqrt(jnp.sum(diagonal, axis=0, keepdims=True))
        x_ref[...] = jnp.where(row_id == col_id, down, 0.0)
        start = g * down * across - eye()
        e_ref[...] = start

        half = n // 2
        top, low = slice(0, half), slice(half, n)

        def subtract_product(fb, xb):
            x_ref[top, top] = x_ref[top, top] - plain(fb[top, top], xb[top, top])
            x_ref[low, top] = x_ref[low, top] - plain(fb[low, :], xb[:, top])
            x_ref[low, low] = x_ref[low, low] - plain(fb[low, low], xb[low, low])

        def rough(state):
            e = e_ref[...]
            f = half_lower(e)
            fb, eb = f.astype(jnp.bfloat16), e.astype(jnp.bfloat16)
            t = jnp.concatenate([plain(fb[top, top], eb[top, :]), plain(fb[low, :], eb)], axis=0)
            w = (f + t - e).astype(jnp.bfloat16)
            left = on_last(w[:, top], fb[top, top]) - t[:, top]
            right = on_last(w, fb[low, :]) - t[:, low]
            e_ref[:, top] = left
            e_ref[:, low] = right
            subtract_product(fb, x_ref[...].astype(jnp.bfloat16))
            return state[0] + 1, jnp.sum(left * left) + jnp.sum(right * right)

        lax.while_loop(lambda s: (s[0] < 12) & (s[1] > small) & (s[1] < 1e6), rough, (0, jnp.sum(start * start)))

        def fine(state):
            x, g = split(x_ref[...]), split(g_ref[...])

            def cut(pair, rows, columns):
                return pair[0][rows, columns], pair[1][rows, columns]

            every = slice(0, n)
            upper = split(triple(plain, cut(x, top, top), cut(g, top, top)))
            lower = split(triple(plain, cut(x, low, every), g))
            first = cut(x, top, top)
            corner = jnp.where(row_id[top, top] == col_id[top, top], 1.0, 0.0)
            e_top = triple(on_last, upper, first) - corner
            e_side = triple(on_last, cut(lower, every, top), first)
            e_low = triple(on_last, lower, cut(x, low, every)) - corner
            f_top, f_low = half_lower(e_top), half_lower(e_low)
            fb = jnp.concatenate(
                [
                    jnp.concatenate([f_top, jnp.zeros_like(f_top)], axis=1),
                    jnp.concatenate([e_side, f_low], axis=1),
                ],
                axis=0,
            ).astype(jnp.bfloat16)
            subtract_product(fb, x[0])
            size = jnp.sum(e_top * e_top) + 2.0 * jnp.sum(e_side * e_side) + jnp.sum(e_low * e_low)
            return state[0] + 1, size

        _, last = lax.while_loop(
            lambda s: (s[0] < 4) & jnp.logical_not(s[1] < enough), fine, (0, jnp.float32(1.0))
        )

        @pl.when(jnp.logical_not(last < enough))
        def _():
            x_ref[...] = eye()
            e_ref[...] = g_ref[...]
            lane = lax.broadcasted_iota(jnp.int32, (1, n), 1)
            below = lax.broadcasted_iota(jnp.int32, (n, 1), 0)

            def eliminate(j, carry):
                row = e_ref[pl.ds(j, 1), :]
                scale = 1.0 / jnp.sqrt(jnp.sum(jnp.where(lane == j, row, 0.0), axis=1, keepdims=True))
                row = jnp.where(lane > j, row * scale, 0.0)
                solved = x_ref[pl.ds(j, 1), :] * scale
                column = jnp.sum(jnp.where(col_id == j, e_ref[...], 0.0), axis=1, keepdims=True) * scale
                column = jnp.where(below > j, column, 0.0)
                e_ref[...] = e_ref[...] - column * row
                x_ref[...] = x_ref[...] - column * solved
                x_ref[pl.ds(j, 1), :] = solved
                return carry

            lax.fori_loop(0, n, eliminate, 0)

        strip_ref[...] = x_ref[pl.ds(pl.multiple_of(here_ref[2] * tile, tile), tile), :]
        for i in range(count):

            @pl.when(here_ref[2] != i)
            def _():
                upto = slice(0, (i + 1) * tile)
                strip = split(x_ref[i * tile : (i + 1) * tile, upto])
                share = split(share_ref[:, upto])
                product = triple(on_last, share, strip)
                for k in range(1, count):

                    @pl.when(here_ref[2] == (i ^ k))
                    def _():
                        out_refs[k - 1][...] = product

    return pl.pallas_call(
        kernel,
        out_shape=[jax.ShapeDtypeStruct((rows, tile), jnp.float32)] * (count - 1)
        + [jax.ShapeDtypeStruct((tile, n), jnp.float32)],
        in_specs=[pl.BlockSpec(memory_space=pltpu.SMEM)] + [pl.BlockSpec(memory_space=pltpu.VMEM)] * (1 + siblings),
        out_specs=[pl.BlockSpec(memory_space=pltpu.VMEM)] * count,
        scratch_shapes=[pltpu.VMEM((height, tile), jnp.float32)] + [pltpu.VMEM((n, n), jnp.float32)] * 3,
        cost_estimate=pl.CostEstimate(flops=12 * n * n * n, bytes_accessed=4 * n * (n + rows), transcendentals=0),
        compiler_params=grant(26),
        name="basis_pieces",
    )(here, *pieces, share)


def own_piece(share, strip):
    rows, n = share.shape
    tile = strip.shape[0]

    def kernel(share_ref, strip_ref, out_ref):
        out_ref[...] = triple(on_last, split(share_ref[...]), split(strip_ref[...]))

    return pl.pallas_call(
        kernel,
        out_shape=jax.ShapeDtypeStruct((rows, tile), jnp.float32),
        in_specs=[pl.BlockSpec(memory_space=pltpu.VMEM)] * 2,
        out_specs=pl.BlockSpec(memory_space=pltpu.VMEM),
        cost_estimate=pl.CostEstimate(flops=6 * rows * n * tile, bytes_accessed=4 * rows * (n + tile), transcendentals=0),
        compiler_params=grant(12),
        name="own_piece",
    )(share, strip)


def lay_out(pieces, here, slots, sub, blk):
    width = pieces[0].shape[1]

    def kernel(here_ref, *refs):
        out_ref, block_ref = refs[-2:]
        for j in range(slots):
            for k in range(len(pieces)):
                spot = pl.ds(pl.multiple_of((here_ref[0] ^ k) * sub, sub), sub)
                block_ref[j, spot, :] = refs[k][j * sub : (j + 1) * sub, :]
        for j in range(slots):
            out_ref[:, j * blk : (j + 1) * blk] = block_ref[j].T

    return pl.pallas_call(
        kernel,
        out_shape=jax.ShapeDtypeStruct((width, slots * blk), jnp.float32),
        in_specs=[pl.BlockSpec(memory_space=pltpu.SMEM)] + [pl.BlockSpec(memory_space=pltpu.VMEM)] * len(pieces),
        out_specs=pl.BlockSpec(memory_space=pltpu.VMEM),
        scratch_shapes=[pltpu.VMEM((slots, blk, width), jnp.float32)],
        compiler_params=grant(12),
        name="lay_out",
    )(here.reshape(1), *pieces)


def shards(child_blocks, sketch, block_map):
    fronts, rows, cols = (lax.axis_size(a) for a in ("front", "row", "col"))
    siblings = min(4, fronts)
    front_here, row_here, col_here = (lax.axis_index(a) for a in ("front", "row", "col"))
    sib_here = front_here % siblings
    total_blocks = block_map.shape[1]
    blocks = total_blocks // rows
    sub = BLK // cols
    sketch_cols = sketch.shape[1]
    parent_blocks = P_SIZE // BLK
    slots = parent_blocks // (siblings * rows)
    spread = parent_blocks - total_blocks
    panel = child_blocks.reshape(blocks, BLK, child_blocks.shape[1])
    both = ("front", "row")

    def place(front, row):
        return front * rows + row

    def may_reach(row, sib, target_row):
        low, high = row * blocks, row * blocks + blocks - 1 + spread
        first = (sib * rows + target_row) * slots
        return low <= first + slots - 1 and first <= high

    maps = [block_map[0]]
    level = 1
    while level < siblings:
        pairs = [(i, i ^ level) for i in range(fronts)]
        maps = maps + [lax.ppermute(m, "front", pairs) for m in maps]
        level *= 2
    own = jnp.stack([lax.dynamic_slice_in_dim(m, row_here * blocks, blocks) for m in maps])
    offset_ids = jnp.arange(rows, dtype=jnp.int32)
    wanted = (sib_here * rows + (row_here ^ offset_ids))[:, None] * slots + jnp.arange(slots, dtype=jnp.int32)[None]
    hit = own[:, None, None, :] == wanted[None, :, :, None]
    inverse = jnp.max(jnp.where(hit, jnp.arange(blocks, dtype=jnp.int32), -1), axis=-1)

    def clipped(dest):
        return jnp.clip(dest, 0, cols - 1)

    wants = []
    for stage in range(1, cols):
        up_dest, down_dest = cols - stage + col_here, stage - cols + col_here
        if stage <= cols // 2:
            wants.append(clipped(jnp.where(up_dest < cols, up_dest, down_dest)))
        else:
            wants += [clipped(up_dest), clipped(down_dest)]
    wants.append(col_here)
    panel = pltpu.with_memory_space_constraint(panel, pltpu.HBM)
    sketch = pltpu.with_memory_space_constraint(sketch, pltpu.HBM)
    ends = (col_here == 0) | (col_here == cols - 1)

    def first_piece(chunk):
        return product_pieces(panel, sketch, wants[:1], sub, COLUMN_CHUNKS, chunk)[0][0]

    def no_piece():
        return jnp.zeros((blocks, sub, sketch_cols // COLUMN_CHUNKS), jnp.float32)

    products = [[lax.cond(ends, lambda h=h: first_piece(h), no_piece) for h in range(COLUMN_CHUNKS)]]
    products += product_pieces(panel, sketch, wants[1:], sub, COLUMN_CHUNKS)

    arrived = []
    for chunk in range(COLUMN_CHUNKS):
        pieces = iter(products)
        came_up = came_down = None
        for stage in range(1, cols):
            up = down = next(pieces)[chunk]
            if stage > cols // 2:
                down = next(pieces)[chunk]
            if came_up is not None:
                up, down = up + came_up, down + came_down
            came_up = lax.ppermute(up, "col", [(i, i + 1) for i in range(stage)])
            came_down = lax.ppermute(down, "col", [(i, i - 1) for i in range(cols - stage, cols)])
        held = [next(pieces)[chunk] + came_up + came_down]
        level = 1
        while level < siblings:
            pairs = [(i, i ^ level) for i in range(fronts)]
            held = held + [lax.ppermute(h, "front", pairs) for h in held]
            level *= 2
        slotted = pack_slots(held, inverse, slots)
        came = [slotted[0]]
        for k in range(1, rows)[::-1]:
            pairs = [
                (place(f, r), place(f, r ^ k))
                for f in range(fronts)
                for r in range(rows)
                if may_reach(r, f % siblings, r ^ k)
            ]
            came.append(lax.ppermute(slotted[k], both, pairs))
        arrived.append(came)

    width = sketch_cols // cols
    here = jnp.stack([sib_here, row_here, col_here])
    share, halves = gram_pieces(arrived, here, siblings, rows, width)

    def swap(x, name, level):
        return lax.ppermute(x, name, [(i, i ^ level) for i in range(lax.axis_size(name))])

    levels = [1 << k for k in range(siblings.bit_length() - 1)]
    kept = dict(enumerate(halves))
    for level in levels:
        kept = {s: kept[s] + swap(kept[s ^ level], "front", level) for s in kept if not s & level}
    parts = kept[0].reshape(rows, kept[0].shape[0] // rows, width)
    piece = parts[0]
    for k in range(1, rows)[::-1]:
        piece = piece + swap(parts[k], "row", k)
    piece = piece + sum(swap(piece, "col", k) for k in range(1, cols)[::-1])
    back = {0: piece}
    for k in range(1, rows)[::-1]:
        back[k] = swap(piece, "row", k)
    pieces = [jnp.concatenate([back[k] for k in range(rows)], axis=0)]
    for level in levels:
        pieces = pieces + [swap(p, "front", level) for p in pieces]

    *basis, strip = basis_pieces(pieces, share, here, rows, width)
    came = {k: swap(basis[k - 1], "col", k) for k in range(1, cols)[::-1]}
    pieces = [own_piece(share, strip)] + [came[k] for k in range(1, cols)]
    return lay_out(pieces, col_here, slots, sub, BLK)


def solution(mesh):
    placed = (P(("front", "row"), "col"), P("col", None), P("front", None))

    return jax.shard_map(shards, mesh=mesh, in_specs=placed, out_specs=P("col", ("front", "row")), check_vma=False)
```

```python
import jax
import jax.numpy as jnp
from jax import lax
from jax.experimental import pallas as pl
from jax.experimental.pallas import tpu as pltpu
from jax.sharding import PartitionSpec as P


P_SIZE = 12288
BLK = 128
COLUMN_CHUNKS = 2


def grant(mebibytes):
    return pltpu.CompilerParams(vmem_limit_bytes=mebibytes << 20)


def product_pieces(panel, sketch, dests, sub, chunks, chunk=None):
    blocks, _, depth = panel.shape
    count = len(dests)
    outs_each = chunks if chunk is None else 1
    width = sketch.shape[1] // chunks
    across = width * outs_each
    step = max(blocks // 2, 1)
    fetches = 4 if step % 4 == 0 else 1
    fetched = step // fetches

    def kernel(dest_ref, *refs):
        a_refs, b_ref, outs = refs[:fetches], refs[fetches], refs[fetches + 1 :]
        a = jnp.concatenate([r[...].reshape(fetched * sub, depth) for r in a_refs], axis=0)
        product = jnp.dot(a, b_ref[...], preferred_element_type=jnp.float32)
        rows = pl.ds(pl.program_id(1) * step, step)
        for k in range(count):

            @pl.when(pl.program_id(0) == k)
            def _():
                for h in range(outs_each):
                    part = product[:, h * width : (h + 1) * width]
                    outs[k * outs_each + h][rows] = part.reshape(step, sub, width)

    outs = pl.pallas_call(
        kernel,
        out_shape=[jax.ShapeDtypeStruct((blocks, sub, width), jnp.float32)] * (count * outs_each),
        grid_spec=pltpu.PrefetchScalarGridSpec(
            num_scalar_prefetch=1,
            grid=(count, blocks // step),
            in_specs=[
                pl.BlockSpec((fetched, sub, depth), lambda p, g, d, i=i: (g * fetches + i, d[p], 0))
                for i in range(fetches)
            ]
            + [
                pl.BlockSpec((depth, across), lambda p, g, d: (0, chunk or 0)),
            ],
            out_specs=[pl.BlockSpec(memory_space=pltpu.VMEM)] * (count * outs_each),
        ),
        cost_estimate=pl.CostEstimate(
            flops=2 * count * blocks * sub * depth * across,
            bytes_accessed=count * blocks * sub * (2 * depth + 4 * across) + 2 * depth * across,
            transcendentals=0,
        ),
        compiler_params=grant(18),
        name="product_pieces",
    )(jnp.stack(dests), *[panel] * fetches, sketch)
    return [outs[k * outs_each : (k + 1) * outs_each] for k in range(count)]


def pack_slots(held, inverse, slots):
    children = len(held)
    offsets = inverse.shape[1]
    _, sub, width = held[0].shape

    def kernel(inv_ref, *refs):
        for o in range(offsets):
            out = refs[children + o]

            def fill(j, carry, o=o, out=out):
                total = jnp.zeros((sub, width), jnp.float32)
                for k in range(children):
                    at = inv_ref[(k * offsets + o) * slots + j]
                    block = refs[k][jnp.maximum(at, 0)]
                    total = total + jnp.where(at >= 0, block, 0.0)
                out[j] = total
                return carry

            lax.fori_loop(0, slots, fill, 0)

    moved = 4 * sub * width * slots * offsets * (children + 1)
    return pl.pallas_call(
        kernel,
        out_shape=[jax.ShapeDtypeStruct((slots, sub, width), jnp.float32)] * offsets,
        in_specs=[pl.BlockSpec(memory_space=pltpu.SMEM)] + [pl.BlockSpec(memory_space=pltpu.VMEM)] * children,
        out_specs=[pl.BlockSpec(memory_space=pltpu.VMEM)] * offsets,
        cost_estimate=pl.CostEstimate(flops=moved, bytes_accessed=moved, transcendentals=0),
        compiler_params=grant(12),
        name="pack_slots",
    )(inverse.reshape(-1), *held)


def on_last(a, b):
    return lax.dot_general(a, b, (((1,), (1,)), ((), ())), preferred_element_type=jnp.float32)


def on_first(a, b):
    return lax.dot_general(a, b, (((0,), (0,)), ((), ())), preferred_element_type=jnp.float32)


def plain(a, b):
    return jnp.dot(a, b, preferred_element_type=jnp.float32)


def split(x):
    high = x.astype(jnp.bfloat16)
    return high, (x - high.astype(jnp.float32)).astype(jnp.bfloat16)


def triple(dot, a, b):
    return dot(a[0], b[0]) + (dot(a[0], b[1]) + dot(a[1], b[0]))


def gram_pieces(arrived, here, siblings, members, tile):
    slots, sub, width = arrived[0][0].shape
    rows, n = slots * sub, width * len(arrived)
    count = n // tile
    height = count * (count + 1) // 2 * tile
    piece = height // (siblings * members)
    counts = [len(a) for a in arrived]

    def kernel(here_ref, *refs):
        inputs, (share_ref, *out_refs, packed_ref) = refs[: sum(counts)], refs[sum(counts) :]
        at = 0
        for h, addends in enumerate(counts):
            share_ref[:, h * width : (h + 1) * width] = sum(r[...] for r in inputs[at : at + addends]).reshape(rows, width)
            at += addends
        high, low = split(share_ref[...])
        at = 0
        for i in range(count):
            here, upto = slice(i * tile, (i + 1) * tile), slice(0, (i + 1) * tile)
            strip = triple(on_first, (high[:, here], low[:, here]), (high[:, upto], low[:, upto]))
            for j in range(i + 1):
                packed_ref[at * tile : (at + 1) * tile, :] = strip[:, j * tile : (j + 1) * tile]
                at += 1
        for s in range(siblings):
            for m in range(members):
                spot = ((here_ref[0] ^ s) * members + (here_ref[1] ^ m)) * piece
                out_refs[s][m * piece : (m + 1) * piece, :] = packed_ref[pl.ds(pl.multiple_of(spot, 8), piece), :]

    flat = [x for a in arrived for x in a]
    outs = pl.pallas_call(
        kernel,
        out_shape=[jax.ShapeDtypeStruct((rows, n), jnp.float32)]
        + [jax.ShapeDtypeStruct((members * piece, tile), jnp.float32)] * siblings,
        in_specs=[pl.BlockSpec(memory_space=pltpu.SMEM)] + [pl.BlockSpec(memory_space=pltpu.VMEM)] * len(flat),
        out_specs=[pl.BlockSpec(memory_space=pltpu.VMEM)] * (1 + siblings),
        scratch_shapes=[pltpu.VMEM((height, tile), jnp.float32)],
        cost_estimate=pl.CostEstimate(
            flops=6 * height * tile * rows, bytes_accessed=4 * (len(flat) + 1) * rows * width, transcendentals=0
        ),
        compiler_params=grant(20),
        name="gram_pieces",
    )(here, *flat)
    return outs[0], list(outs[1:])


def basis_pieces(pieces, share, here, members, tile):
    rows, n = share.shape
    count = n // tile
    siblings = len(pieces)
    height = count * (count + 1) // 2 * tile
    piece = height // (siblings * members)
    small, enough = 1e-2, 4e-4

    def kernel(here_ref, *refs):
        piece_refs, share_ref = refs[:siblings], refs[siblings]
        out_refs, strip_ref = refs[siblings + 1 : -5], refs[-5]
        packed_ref, g_ref, x_ref, e_ref = refs[-4:]
        for s in range(siblings):
            for m in range(members):
                spot = ((here_ref[0] ^ s) * members + (here_ref[1] ^ m)) * piece
                packed_ref[pl.ds(pl.multiple_of(spot, 8), piece), :] = piece_refs[s][m * piece : (m + 1) * piece, :]
        at = 0
        for i in range(count):
            here = slice(i * tile, (i + 1) * tile)
            for j in range(i + 1):
                there = slice(j * tile, (j + 1) * tile)
                block = packed_ref[at * tile : (at + 1) * tile, :]
                g_ref[here, there] = block
                if j < i:
                    g_ref[there, here] = block.T
                at += 1
        row_id = lax.broadcasted_iota(jnp.int32, (n, n), 0)
        col_id = lax.broadcasted_iota(jnp.int32, (n, n), 1)

        def eye():
            return jnp.where(row_id == col_id, 1.0, 0.0)

        def half_lower(e):
            rows, columns = row_id[: e.shape[0], : e.shape[1]], col_id[: e.shape[0], : e.shape[1]]
            return jnp.where(rows > columns, e, jnp.where(rows == columns, 0.5 * e, 0.0))

        g = g_ref[...]
        diagonal = jnp.where(row_id == col_id, g, 0.0)
        down = 1.0 / jnp.sqrt(jnp.sum(diagonal, axis=1, keepdims=True))
        across = 1.0 / jnp.sqrt(jnp.sum(diagonal, axis=0, keepdims=True))
        x_ref[...] = jnp.where(row_id == col_id, down, 0.0)
        start = g * down * across - eye()
        e_ref[...] = start

        half = n // 2
        top, low = slice(0, half), slice(half, n)

        def subtract_product(fb, xb):
            x_ref[top, top] = x_ref[top, top] - plain(fb[top, top], xb[top, top])
            x_ref[low, top] = x_ref[low, top] - plain(fb[low, :], xb[:, top])
            x_ref[low, low] = x_ref[low, low] - plain(fb[low, low], xb[low, low])

        def rough(state):
            e = e_ref[...]
            f = half_lower(e)
            fb, eb = f.astype(jnp.bfloat16), e.astype(jnp.bfloat16)
            t = jnp.concatenate([plain(fb[top, top], eb[top, :]), plain(fb[low, :], eb)], axis=0)
            w = (f + t - e).astype(jnp.bfloat16)
            left = on_last(w[:, top], fb[top, top]) - t[:, top]
            right = on_last(w, fb[low, :]) - t[:, low]
            e_ref[:, top] = left
            e_ref[:, low] = right
            subtract_product(fb, x_ref[...].astype(jnp.bfloat16))
            return state[0] + 1, jnp.sum(left * left) + jnp.sum(right * right)

        lax.while_loop(lambda s: (s[0] < 12) & (s[1] > small) & (s[1] < 1e6), rough, (0, jnp.sum(start * start)))

        def fine(state):
            x, g = split(x_ref[...]), split(g_ref[...])

            def cut(pair, rows, columns):
                return pair[0][rows, columns], pair[1][rows, columns]

            every = slice(0, n)
            upper = split(triple(plain, cut(x, top, top), cut(g, top, top)))
            lower = split(triple(plain, cut(x, low, every), g))
            first = cut(x, top, top)
            corner = jnp.where(row_id[top, top] == col_id[top, top], 1.0, 0.0)
            e_top = triple(on_last, upper, first) - corner
            e_side = triple(on_last, cut(lower, every, top), first)
            e_low = triple(on_last, lower, cut(x, low, every)) - corner
            f_top, f_low = half_lower(e_top), half_lower(e_low)
            fb = jnp.concatenate(
                [
                    jnp.concatenate([f_top, jnp.zeros_like(f_top)], axis=1),
                    jnp.concatenate([e_side, f_low], axis=1),
                ],
                axis=0,
            ).astype(jnp.bfloat16)
            subtract_product(fb, x[0])
            size = jnp.sum(e_top * e_top) + 2.0 * jnp.sum(e_side * e_side) + jnp.sum(e_low * e_low)
            return state[0] + 1, size

        _, last = lax.while_loop(
            lambda s: (s[0] < 4) & jnp.logical_not(s[1] < enough), fine, (0, jnp.float32(1.0))
        )

        @pl.when(jnp.logical_not(last < enough))
        def _():
            x_ref[...] = eye()
            e_ref[...] = g_ref[...]
            lane = lax.broadcasted_iota(jnp.int32, (1, n), 1)
            below = lax.broadcasted_iota(jnp.int32, (n, 1), 0)

            def eliminate(j, carry):
                row = e_ref[pl.ds(j, 1), :]
                scale = 1.0 / jnp.sqrt(jnp.sum(jnp.where(lane == j, row, 0.0), axis=1, keepdims=True))
                row = jnp.where(lane > j, row * scale, 0.0)
                solved = x_ref[pl.ds(j, 1), :] * scale
                column = jnp.sum(jnp.where(col_id == j, e_ref[...], 0.0), axis=1, keepdims=True) * scale
                column = jnp.where(below > j, column, 0.0)
                e_ref[...] = e_ref[...] - column * row
                x_ref[...] = x_ref[...] - column * solved
                x_ref[pl.ds(j, 1), :] = solved
                return carry

            lax.fori_loop(0, n, eliminate, 0)

        strip_ref[...] = x_ref[pl.ds(pl.multiple_of(here_ref[2] * tile, tile), tile), :]
        for i in range(count):

            @pl.when(here_ref[2] != i)
            def _():
                upto = slice(0, (i + 1) * tile)
                strip = split(x_ref[i * tile : (i + 1) * tile, upto])
                share = split(share_ref[:, upto])
                product = triple(on_last, share, strip)
                for k in range(1, count):

                    @pl.when(here_ref[2] == (i ^ k))
                    def _():
                        out_refs[k - 1][...] = product

    return pl.pallas_call(
        kernel,
        out_shape=[jax.ShapeDtypeStruct((rows, tile), jnp.float32)] * (count - 1)
        + [jax.ShapeDtypeStruct((tile, n), jnp.float32)],
        in_specs=[pl.BlockSpec(memory_space=pltpu.SMEM)] + [pl.BlockSpec(memory_space=pltpu.VMEM)] * (1 + siblings),
        out_specs=[pl.BlockSpec(memory_space=pltpu.VMEM)] * count,
        scratch_shapes=[pltpu.VMEM((height, tile), jnp.float32)] + [pltpu.VMEM((n, n), jnp.float32)] * 3,
        cost_estimate=pl.CostEstimate(flops=12 * n * n * n, bytes_accessed=4 * n * (n + rows), transcendentals=0),
        compiler_params=grant(26),
        name="basis_pieces",
    )(here, *pieces, share)


def own_piece(share, strip):
    rows, n = share.shape
    tile = strip.shape[0]

    def kernel(share_ref, strip_ref, out_ref):
        out_ref[...] = triple(on_last, split(share_ref[...]), split(strip_ref[...]))

    return pl.pallas_call(
        kernel,
        out_shape=jax.ShapeDtypeStruct((rows, tile), jnp.float32),
        in_specs=[pl.BlockSpec(memory_space=pltpu.VMEM)] * 2,
        out_specs=pl.BlockSpec(memory_space=pltpu.VMEM),
        cost_estimate=pl.CostEstimate(flops=6 * rows * n * tile, bytes_accessed=4 * rows * (n + tile), transcendentals=0),
        compiler_params=grant(12),
        name="own_piece",
    )(share, strip)


def lay_out(pieces, here, slots, sub, blk):
    width = pieces[0].shape[1]

    def kernel(here_ref, *refs):
        out_ref, block_ref = refs[-2:]
        for j in range(slots):
            for k in range(len(pieces)):
                spot = pl.ds(pl.multiple_of((here_ref[0] ^ k) * sub, sub), sub)
                block_ref[j, spot, :] = refs[k][j * sub : (j + 1) * sub, :]
        for j in range(slots):
            out_ref[:, j * blk : (j + 1) * blk] = block_ref[j].T

    return pl.pallas_call(
        kernel,
        out_shape=jax.ShapeDtypeStruct((width, slots * blk), jnp.float32),
        in_specs=[pl.BlockSpec(memory_space=pltpu.SMEM)] + [pl.BlockSpec(memory_space=pltpu.VMEM)] * len(pieces),
        out_specs=pl.BlockSpec(memory_space=pltpu.VMEM),
        scratch_shapes=[pltpu.VMEM((slots, blk, width), jnp.float32)],
        compiler_params=grant(12),
        name="lay_out",
    )(here.reshape(1), *pieces)


def shards(child_blocks, sketch, block_map):
    fronts, rows, cols = (lax.axis_size(a) for a in ("front", "row", "col"))
    siblings = min(4, fronts)
    front_here, row_here, col_here = (lax.axis_index(a) for a in ("front", "row", "col"))
    sib_here = front_here % siblings
    total_blocks = block_map.shape[1]
    blocks = total_blocks // rows
    sub = BLK // cols
    sketch_cols = sketch.shape[1]
    parent_blocks = P_SIZE // BLK
    slots = parent_blocks // (siblings * rows)
    spread = parent_blocks - total_blocks
    panel = child_blocks.reshape(blocks, BLK, child_blocks.shape[1])
    both = ("front", "row")

    def place(front, row):
        return front * rows + row

    def may_reach(row, sib, target_row):
        low, high = row * blocks, row * blocks + blocks - 1 + spread
        first = (sib * rows + target_row) * slots
        return low <= first + slots - 1 and first <= high

    maps = [block_map[0]]
    level = 1
    while level < siblings:
        pairs = [(i, i ^ level) for i in range(fronts)]
        maps = maps + [lax.ppermute(m, "front", pairs) for m in maps]
        level *= 2
    own = jnp.stack([lax.dynamic_slice_in_dim(m, row_here * blocks, blocks) for m in maps])
    offset_ids = jnp.arange(rows, dtype=jnp.int32)
    wanted = (sib_here * rows + (row_here ^ offset_ids))[:, None] * slots + jnp.arange(slots, dtype=jnp.int32)[None]
    hit = own[:, None, None, :] == wanted[None, :, :, None]
    inverse = jnp.max(jnp.where(hit, jnp.arange(blocks, dtype=jnp.int32), -1), axis=-1)

    def clipped(dest):
        return jnp.clip(dest, 0, cols - 1)

    wants = []
    for stage in range(1, cols):
        up_dest, down_dest = cols - stage + col_here, stage - cols + col_here
        if stage <= cols // 2:
            wants.append(clipped(jnp.where(up_dest < cols, up_dest, down_dest)))
        else:
            wants += [clipped(up_dest), clipped(down_dest)]
    wants.append(col_here)
    panel = pltpu.with_memory_space_constraint(panel, pltpu.HBM)
    sketch = pltpu.with_memory_space_constraint(sketch, pltpu.HBM)
    ends = (col_here == 0) | (col_here == cols - 1)

    def first_piece(chunk):
        return product_pieces(panel, sketch, wants[:1], sub, COLUMN_CHUNKS, chunk)[0][0]

    def no_piece():
        return jnp.zeros((blocks, sub, sketch_cols // COLUMN_CHUNKS), jnp.float32)

    products = [[lax.cond(ends, lambda h=h: first_piece(h), no_piece) for h in range(COLUMN_CHUNKS)]]
    products += product_pieces(panel, sketch, wants[1:], sub, COLUMN_CHUNKS)

    arrived = []
    for chunk in range(COLUMN_CHUNKS):
        pieces = iter(products)
        came_up = came_down = None
        for stage in range(1, cols):
            up = down = next(pieces)[chunk]
            if stage > cols // 2:
                down = next(pieces)[chunk]
            if came_up is not None and came_up is came_down:
                up = down = up + came_up
            elif came_up is not None:
                up, down = up + came_up, down + came_down
            if stage == 1 and cols > 3:
                came_up = came_down = lax.ppermute(up, "col", [(0, 1), (cols - 1, cols - 2)])
                continue
            came_up = lax.ppermute(up, "col", [(i, i + 1) for i in range(stage)])
            came_down = lax.ppermute(down, "col", [(i, i - 1) for i in range(cols - stage, cols)])
        held = [next(pieces)[chunk] + came_up + came_down]
        level = 1
        while level < siblings:
            pairs = [(i, i ^ level) for i in range(fronts)]
            held = held + [lax.ppermute(h, "front", pairs) for h in held]
            level *= 2
        slotted = pack_slots(held, inverse, slots)
        came = [slotted[0]]
        for k in range(1, rows)[::-1]:
            pairs = [
                (place(f, r), place(f, r ^ k))
                for f in range(fronts)
                for r in range(rows)
                if may_reach(r, f % siblings, r ^ k)
            ]
            came.append(lax.ppermute(slotted[k], both, pairs))
        arrived.append(came)

    width = sketch_cols // cols
    here = jnp.stack([sib_here, row_here, col_here])
    share, halves = gram_pieces(arrived, here, siblings, rows, width)

    def swap(x, name, level):
        return lax.ppermute(x, name, [(i, i ^ level) for i in range(lax.axis_size(name))])

    levels = [1 << k for k in range(siblings.bit_length() - 1)]
    kept = dict(enumerate(halves))
    for level in levels:
        kept = {s: kept[s] + swap(kept[s ^ level], "front", level) for s in kept if not s & level}
    parts = kept[0].reshape(rows, kept[0].shape[0] // rows, width)
    piece = parts[0]
    for k in range(1, rows)[::-1]:
        piece = piece + swap(parts[k], "row", k)
    piece = piece + sum(swap(piece, "col", k) for k in range(1, cols)[::-1])
    back = {0: piece}
    for k in range(1, rows)[::-1]:
        back[k] = swap(piece, "row", k)
    pieces = [jnp.concatenate([back[k] for k in range(rows)], axis=0)]
    for level in levels:
        pieces = pieces + [swap(p, "front", level) for p in pieces]

    *basis, strip = basis_pieces(pieces, share, here, rows, width)
    came = {k: swap(basis[k - 1], "col", k) for k in range(1, cols)[::-1]}
    pieces = [own_piece(share, strip)] + [came[k] for k in range(1, cols)]
    return lay_out(pieces, col_here, slots, sub, BLK)


def solution(mesh):
    placed = (P(("front", "row"), "col"), P("col", None), P("front", None))

    return jax.shard_map(shards, mesh=mesh, in_specs=placed, out_specs=P("col", ("front", "row")), check_vma=False)
```

```python
import jax
import jax.numpy as jnp
from jax import lax
from jax.experimental import pallas as pl
from jax.experimental.pallas import tpu as pltpu
from jax.sharding import PartitionSpec as P


P_SIZE = 12288
BLK = 128
COLUMN_CHUNKS = 2


def grant(mebibytes):
    return pltpu.CompilerParams(vmem_limit_bytes=mebibytes << 20)


def product_pieces(panel, sketch, dests, sub, chunks, chunk=None):
    blocks, _, depth = panel.shape
    count = len(dests)
    outs_each = chunks if chunk is None else 1
    width = sketch.shape[1] // chunks
    across = width * outs_each
    step = max(blocks // 2, 1)
    fetches = 4 if step % 4 == 0 else 1
    fetched = step // fetches

    def kernel(dest_ref, *refs):
        a_refs, b_ref, outs = refs[:fetches], refs[fetches], refs[fetches + 1 :]
        a = jnp.concatenate([r[...].reshape(fetched * sub, depth) for r in a_refs], axis=0)
        product = jnp.dot(a, b_ref[...], preferred_element_type=jnp.float32)
        rows = pl.ds(pl.program_id(1) * step, step)
        for k in range(count):

            @pl.when(pl.program_id(0) == k)
            def _():
                for h in range(outs_each):
                    part = product[:, h * width : (h + 1) * width]
                    outs[k * outs_each + h][rows] = part.reshape(step, sub, width)

    outs = pl.pallas_call(
        kernel,
        out_shape=[jax.ShapeDtypeStruct((blocks, sub, width), jnp.float32)] * (count * outs_each),
        grid_spec=pltpu.PrefetchScalarGridSpec(
            num_scalar_prefetch=1,
            grid=(count, blocks // step),
            in_specs=[
                pl.BlockSpec((fetched, sub, depth), lambda p, g, d, i=i: (g * fetches + i, d[p], 0))
                for i in range(fetches)
            ]
            + [
                pl.BlockSpec((depth, across), lambda p, g, d: (0, chunk or 0)),
            ],
            out_specs=[pl.BlockSpec(memory_space=pltpu.VMEM)] * (count * outs_each),
        ),
        cost_estimate=pl.CostEstimate(
            flops=2 * count * blocks * sub * depth * across,
            bytes_accessed=count * blocks * sub * (2 * depth + 4 * across) + 2 * depth * across,
            transcendentals=0,
        ),
        compiler_params=grant(18),
        name="product_pieces",
    )(jnp.stack(dests), *[panel] * fetches, sketch)
    return [outs[k * outs_each : (k + 1) * outs_each] for k in range(count)]


def pack_slots(held, inverse, slots):
    children = len(held)
    offsets = inverse.shape[1]
    _, sub, width = held[0].shape

    def kernel(inv_ref, *refs):
        for o in range(offsets):
            out = refs[children + o]

            def fill(j, carry, o=o, out=out):
                total = jnp.zeros((sub, width), jnp.float32)
                for k in range(children):
                    at = inv_ref[(k * offsets + o) * slots + j]
                    block = refs[k][jnp.maximum(at, 0)]
                    total = total + jnp.where(at >= 0, block, 0.0)
                out[j] = total
                return carry

            lax.fori_loop(0, slots, fill, 0)

    moved = 4 * sub * width * slots * offsets * (children + 1)
    return pl.pallas_call(
        kernel,
        out_shape=[jax.ShapeDtypeStruct((slots, sub, width), jnp.float32)] * offsets,
        in_specs=[pl.BlockSpec(memory_space=pltpu.SMEM)] + [pl.BlockSpec(memory_space=pltpu.VMEM)] * children,
        out_specs=[pl.BlockSpec(memory_space=pltpu.VMEM)] * offsets,
        cost_estimate=pl.CostEstimate(flops=moved, bytes_accessed=moved, transcendentals=0),
        compiler_params=grant(8),
        name="pack_slots",
    )(inverse.reshape(-1), *held)


def on_last(a, b):
    return lax.dot_general(a, b, (((1,), (1,)), ((), ())), preferred_element_type=jnp.float32)


def on_first(a, b):
    return lax.dot_general(a, b, (((0,), (0,)), ((), ())), preferred_element_type=jnp.float32)


def plain(a, b):
    return jnp.dot(a, b, preferred_element_type=jnp.float32)


def split(x):
    high = x.astype(jnp.bfloat16)
    return high, (x - high.astype(jnp.float32)).astype(jnp.bfloat16)


def triple(dot, a, b):
    return dot(a[0], b[0]) + (dot(a[0], b[1]) + dot(a[1], b[0]))


def gram_pieces(arrived, here, siblings, members, tile):
    slots, sub, width = arrived[0][0].shape
    rows, n = slots * sub, width * len(arrived)
    count = n // tile
    height = count * (count + 1) // 2 * tile
    piece = height // (siblings * members)
    counts = [len(a) for a in arrived]

    def kernel(here_ref, *refs):
        inputs, (share_ref, *out_refs, packed_ref) = refs[: sum(counts)], refs[sum(counts) :]
        at = 0
        for h, addends in enumerate(counts):
            share_ref[:, h * width : (h + 1) * width] = sum(r[...] for r in inputs[at : at + addends]).reshape(rows, width)
            at += addends
        high, low = split(share_ref[...])
        at = 0
        for i in range(count):
            here, upto = slice(i * tile, (i + 1) * tile), slice(0, (i + 1) * tile)
            strip = triple(on_first, (high[:, here], low[:, here]), (high[:, upto], low[:, upto]))
            for j in range(i + 1):
                packed_ref[at * tile : (at + 1) * tile, :] = strip[:, j * tile : (j + 1) * tile]
                at += 1
        for s in range(siblings):
            for m in range(members):
                spot = ((here_ref[0] ^ s) * members + (here_ref[1] ^ m)) * piece
                out_refs[s][m * piece : (m + 1) * piece, :] = packed_ref[pl.ds(pl.multiple_of(spot, 8), piece), :]

    flat = [x for a in arrived for x in a]
    outs = pl.pallas_call(
        kernel,
        out_shape=[jax.ShapeDtypeStruct((rows, n), jnp.float32)]
        + [jax.ShapeDtypeStruct((members * piece, tile), jnp.float32)] * siblings,
        in_specs=[pl.BlockSpec(memory_space=pltpu.SMEM)] + [pl.BlockSpec(memory_space=pltpu.VMEM)] * len(flat),
        out_specs=[pl.BlockSpec(memory_space=pltpu.VMEM)] * (1 + siblings),
        scratch_shapes=[pltpu.VMEM((height, tile), jnp.float32)],
        cost_estimate=pl.CostEstimate(
            flops=6 * height * tile * rows, bytes_accessed=4 * (len(flat) + 1) * rows * width, transcendentals=0
        ),
        compiler_params=grant(14),
        name="gram_pieces",
    )(here, *flat)
    return outs[0], list(outs[1:])


def basis_pieces(pieces, share, here, members, tile):
    rows, n = share.shape
    count = n // tile
    siblings = len(pieces)
    height = count * (count + 1) // 2 * tile
    piece = height // (siblings * members)
    small, enough = 1e-2, 4e-4

    def kernel(here_ref, *refs):
        piece_refs, share_ref = refs[:siblings], refs[siblings]
        out_refs, strip_ref = refs[siblings + 1 : -5], refs[-5]
        packed_ref, g_ref, x_ref, e_ref = refs[-4:]
        for s in range(siblings):
            for m in range(members):
                spot = ((here_ref[0] ^ s) * members + (here_ref[1] ^ m)) * piece
                packed_ref[pl.ds(pl.multiple_of(spot, 8), piece), :] = piece_refs[s][m * piece : (m + 1) * piece, :]
        at = 0
        for i in range(count):
            here = slice(i * tile, (i + 1) * tile)
            for j in range(i + 1):
                there = slice(j * tile, (j + 1) * tile)
                block = packed_ref[at * tile : (at + 1) * tile, :]
                g_ref[here, there] = block
                if j < i:
                    g_ref[there, here] = block.T
                at += 1
        row_id = lax.broadcasted_iota(jnp.int32, (n, n), 0)
        col_id = lax.broadcasted_iota(jnp.int32, (n, n), 1)

        def eye():
            return jnp.where(row_id == col_id, 1.0, 0.0)

        def half_lower(e):
            rows, columns = row_id[: e.shape[0], : e.shape[1]], col_id[: e.shape[0], : e.shape[1]]
            return jnp.where(rows > columns, e, jnp.where(rows == columns, 0.5 * e, 0.0))

        g = g_ref[...]
        diagonal = jnp.where(row_id == col_id, g, 0.0)
        down = 1.0 / jnp.sqrt(jnp.sum(diagonal, axis=1, keepdims=True))
        across = 1.0 / jnp.sqrt(jnp.sum(diagonal, axis=0, keepdims=True))
        x_ref[...] = jnp.where(row_id == col_id, down, 0.0)
        start = g * down * across - eye()
        e_ref[...] = start

        half = n // 2
        top, low = slice(0, half), slice(half, n)

        def subtract_product(fb, xb):
            x_ref[top, top] = x_ref[top, top] - plain(fb[top, top], xb[top, top])
            x_ref[low, top] = x_ref[low, top] - plain(fb[low, :], xb[:, top])
            x_ref[low, low] = x_ref[low, low] - plain(fb[low, low], xb[low, low])

        def rough(state):
            e = e_ref[...]
            f = half_lower(e)
            fb, eb = f.astype(jnp.bfloat16), e.astype(jnp.bfloat16)
            t = jnp.concatenate([plain(fb[top, top], eb[top, :]), plain(fb[low, :], eb)], axis=0)
            w = (f + t - e).astype(jnp.bfloat16)
            left = on_last(w[:, top], fb[top, top]) - t[:, top]
            right = on_last(w, fb[low, :]) - t[:, low]
            e_ref[:, top] = left
            e_ref[:, low] = right
            subtract_product(fb, x_ref[...].astype(jnp.bfloat16))
            return state[0] + 1, jnp.sum(left * left) + jnp.sum(right * right)

        lax.while_loop(lambda s: (s[0] < 12) & (s[1] > small) & (s[1] < 1e6), rough, (0, jnp.sum(start * start)))

        def fine(state):
            x, g = split(x_ref[...]), split(g_ref[...])

            def cut(pair, rows, columns):
                return pair[0][rows, columns], pair[1][rows, columns]

            every = slice(0, n)
            upper = split(triple(plain, cut(x, top, top), cut(g, top, top)))
            lower = split(triple(plain, cut(x, low, every), g))
            first = cut(x, top, top)
            corner = jnp.where(row_id[top, top] == col_id[top, top], 1.0, 0.0)
            e_top = triple(on_last, upper, first) - corner
            e_side = triple(on_last, cut(lower, every, top), first)
            e_low = triple(on_last, lower, cut(x, low, every)) - corner
            f_top, f_low = half_lower(e_top), half_lower(e_low)
            fb = jnp.concatenate(
                [
                    jnp.concatenate([f_top, jnp.zeros_like(f_top)], axis=1),
                    jnp.concatenate([e_side, f_low], axis=1),
                ],
                axis=0,
            ).astype(jnp.bfloat16)
            subtract_product(fb, x[0])
            size = jnp.sum(e_top * e_top) + 2.0 * jnp.sum(e_side * e_side) + jnp.sum(e_low * e_low)
            return state[0] + 1, size

        _, last = lax.while_loop(
            lambda s: (s[0] < 4) & jnp.logical_not(s[1] < enough), fine, (0, jnp.float32(1.0))
        )

        @pl.when(jnp.logical_not(last < enough))
        def _():
            x_ref[...] = eye()
            e_ref[...] = g_ref[...]
            lane = lax.broadcasted_iota(jnp.int32, (1, n), 1)
            below = lax.broadcasted_iota(jnp.int32, (n, 1), 0)

            def eliminate(j, carry):
                row = e_ref[pl.ds(j, 1), :]
                scale = 1.0 / jnp.sqrt(jnp.sum(jnp.where(lane == j, row, 0.0), axis=1, keepdims=True))
                row = jnp.where(lane > j, row * scale, 0.0)
                solved = x_ref[pl.ds(j, 1), :] * scale
                column = jnp.sum(jnp.where(col_id == j, e_ref[...], 0.0), axis=1, keepdims=True) * scale
                column = jnp.where(below > j, column, 0.0)
                e_ref[...] = e_ref[...] - column * row
                x_ref[...] = x_ref[...] - column * solved
                x_ref[pl.ds(j, 1), :] = solved
                return carry

            lax.fori_loop(0, n, eliminate, 0)

        strip_ref[...] = x_ref[pl.ds(pl.multiple_of(here_ref[2] * tile, tile), tile), :]
        for i in range(count):

            @pl.when(here_ref[2] != i)
            def _():
                upto = slice(0, (i + 1) * tile)
                strip = split(x_ref[i * tile : (i + 1) * tile, upto])
                share = split(share_ref[:, upto])
                product = triple(on_last, share, strip)
                for k in range(1, count):

                    @pl.when(here_ref[2] == (i ^ k))
                    def _():
                        out_refs[k - 1][...] = product

    return pl.pallas_call(
        kernel,
        out_shape=[jax.ShapeDtypeStruct((rows, tile), jnp.float32)] * (count - 1)
        + [jax.ShapeDtypeStruct((tile, n), jnp.float32)],
        in_specs=[pl.BlockSpec(memory_space=pltpu.SMEM)] + [pl.BlockSpec(memory_space=pltpu.VMEM)] * (1 + siblings),
        out_specs=[pl.BlockSpec(memory_space=pltpu.VMEM)] * count,
        scratch_shapes=[pltpu.VMEM((height, tile), jnp.float32)] + [pltpu.VMEM((n, n), jnp.float32)] * 3,
        cost_estimate=pl.CostEstimate(flops=12 * n * n * n, bytes_accessed=4 * n * (n + rows), transcendentals=0),
        compiler_params=grant(26),
        name="basis_pieces",
    )(here, *pieces, share)


def own_piece(share, strip):
    rows, n = share.shape
    tile = strip.shape[0]

    def kernel(share_ref, strip_ref, out_ref):
        out_ref[...] = triple(on_last, split(share_ref[...]), split(strip_ref[...]))

    return pl.pallas_call(
        kernel,
        out_shape=jax.ShapeDtypeStruct((rows, tile), jnp.float32),
        in_specs=[pl.BlockSpec(memory_space=pltpu.VMEM)] * 2,
        out_specs=pl.BlockSpec(memory_space=pltpu.VMEM),
        cost_estimate=pl.CostEstimate(flops=6 * rows * n * tile, bytes_accessed=4 * rows * (n + tile), transcendentals=0),
        compiler_params=grant(8),
        name="own_piece",
    )(share, strip)


def lay_out(pieces, here, slots, sub, blk):
    width = pieces[0].shape[1]

    def kernel(here_ref, *refs):
        out_ref, block_ref = refs[-2:]
        for j in range(slots):
            for k in range(len(pieces)):
                spot = pl.ds(pl.multiple_of((here_ref[0] ^ k) * sub, sub), sub)
                block_ref[j, spot, :] = refs[k][j * sub : (j + 1) * sub, :]
        for j in range(slots):
            out_ref[:, j * blk : (j + 1) * blk] = block_ref[j].T

    return pl.pallas_call(
        kernel,
        out_shape=jax.ShapeDtypeStruct((width, slots * blk), jnp.float32),
        in_specs=[pl.BlockSpec(memory_space=pltpu.SMEM)] + [pl.BlockSpec(memory_space=pltpu.VMEM)] * len(pieces),
        out_specs=pl.BlockSpec(memory_space=pltpu.VMEM),
        scratch_shapes=[pltpu.VMEM((slots, blk, width), jnp.float32)],
        compiler_params=grant(8),
        name="lay_out",
    )(here.reshape(1), *pieces)


def shards(child_blocks, sketch, block_map):
    fronts, rows, cols = (lax.axis_size(a) for a in ("front", "row", "col"))
    siblings = min(4, fronts)
    front_here, row_here, col_here = (lax.axis_index(a) for a in ("front", "row", "col"))
    sib_here = front_here % siblings
    total_blocks = block_map.shape[1]
    blocks = total_blocks // rows
    sub = BLK // cols
    sketch_cols = sketch.shape[1]
    parent_blocks = P_SIZE // BLK
    slots = parent_blocks // (siblings * rows)
    spread = parent_blocks - total_blocks
    panel = child_blocks.reshape(blocks, BLK, child_blocks.shape[1])
    both = ("front", "row")

    def place(front, row):
        return front * rows + row

    def may_reach(row, sib, target_row):
        low, high = row * blocks, row * blocks + blocks - 1 + spread
        first = (sib * rows + target_row) * slots
        return low <= first + slots - 1 and first <= high

    maps = [block_map[0]]
    level = 1
    while level < siblings:
        pairs = [(i, i ^ level) for i in range(fronts)]
        maps = maps + [lax.ppermute(m, "front", pairs) for m in maps]
        level *= 2
    own = jnp.stack([lax.dynamic_slice_in_dim(m, row_here * blocks, blocks) for m in maps])
    offset_ids = jnp.arange(rows, dtype=jnp.int32)
    wanted = (sib_here * rows + (row_here ^ offset_ids))[:, None] * slots + jnp.arange(slots, dtype=jnp.int32)[None]
    hit = own[:, None, None, :] == wanted[None, :, :, None]
    inverse = jnp.max(jnp.where(hit, jnp.arange(blocks, dtype=jnp.int32), -1), axis=-1)

    def clipped(dest):
        return jnp.clip(dest, 0, cols - 1)

    wants = []
    for stage in range(1, cols):
        up_dest, down_dest = cols - stage + col_here, stage - cols + col_here
        if stage <= cols // 2:
            wants.append(clipped(jnp.where(up_dest < cols, up_dest, down_dest)))
        else:
            wants += [clipped(up_dest), clipped(down_dest)]
    wants.append(col_here)
    panel = pltpu.with_memory_space_constraint(panel, pltpu.HBM)
    sketch = pltpu.with_memory_space_constraint(sketch, pltpu.HBM)
    ends = (col_here == 0) | (col_here == cols - 1)

    def first_piece(chunk):
        return product_pieces(panel, sketch, wants[:1], sub, COLUMN_CHUNKS, chunk)[0][0]

    def no_piece():
        return jnp.zeros((blocks, sub, sketch_cols // COLUMN_CHUNKS), jnp.float32)

    products = [[lax.cond(ends, lambda h=h: first_piece(h), no_piece) for h in range(COLUMN_CHUNKS)]]
    products += product_pieces(panel, sketch, wants[1:], sub, COLUMN_CHUNKS)

    arrived = []
    for chunk in range(COLUMN_CHUNKS):
        pieces = iter(products)
        came_up = came_down = None
        for stage in range(1, cols):
            up = down = next(pieces)[chunk]
            if stage > cols // 2:
                down = next(pieces)[chunk]
            if came_up is not None and came_up is came_down:
                up = down = up + came_up
            elif came_up is not None:
                up, down = up + came_up, down + came_down
            if stage == 1 and cols > 3:
                came_up = came_down = lax.ppermute(up, "col", [(0, 1), (cols - 1, cols - 2)])
                continue
            came_up = lax.ppermute(up, "col", [(i, i + 1) for i in range(stage)])
            came_down = lax.ppermute(down, "col", [(i, i - 1) for i in range(cols - stage, cols)])
        held = [next(pieces)[chunk] + came_up + came_down]
        level = 1
        while level < siblings:
            pairs = [(i, i ^ level) for i in range(fronts)]
            held = held + [lax.ppermute(h, "front", pairs) for h in held]
            level *= 2
        slotted = pack_slots(held, inverse, slots)
        came = [slotted[0]]
        for k in range(1, rows)[::-1]:
            pairs = [
                (place(f, r), place(f, r ^ k))
                for f in range(fronts)
                for r in range(rows)
                if may_reach(r, f % siblings, r ^ k)
            ]
            came.append(lax.ppermute(slotted[k], both, pairs))
        arrived.append(came)

    width = sketch_cols // cols
    here = jnp.stack([sib_here, row_here, col_here])
    share, halves = gram_pieces(arrived, here, siblings, rows, width)

    def swap(x, name, level):
        return lax.ppermute(x, name, [(i, i ^ level) for i in range(lax.axis_size(name))])

    levels = [1 << k for k in range(siblings.bit_length() - 1)]
    kept = dict(enumerate(halves))
    for level in levels:
        kept = {s: kept[s] + swap(kept[s ^ level], "front", level) for s in kept if not s & level}
    parts = kept[0].reshape(rows, kept[0].shape[0] // rows, width)
    piece = parts[0]
    for k in range(1, rows)[::-1]:
        piece = piece + swap(parts[k], "row", k)
    piece = piece + sum(swap(piece, "col", k) for k in range(1, cols)[::-1])
    back = {0: piece}
    for k in range(1, rows)[::-1]:
        back[k] = swap(piece, "row", k)
    pieces = [jnp.concatenate([back[k] for k in range(rows)], axis=0)]
    for level in levels:
        pieces = pieces + [swap(p, "front", level) for p in pieces]

    *basis, strip = basis_pieces(pieces, share, here, rows, width)
    came = {k: swap(basis[k - 1], "col", k) for k in range(1, cols)[::-1]}
    pieces = [own_piece(share, strip)] + [came[k] for k in range(1, cols)]
    return lay_out(pieces, col_here, slots, sub, BLK)


def solution(mesh):
    placed = (P(("front", "row"), "col"), P("col", None), P("front", None))

    return jax.shard_map(shards, mesh=mesh, in_specs=placed, out_specs=P("col", ("front", "row")), check_vma=False)
```
